256 devices in a mesh: seq: 32 (over y, z), head: 4 (over x), dp: 2 (over core).
Axes of the slice: x: 4, y: 4, z: 8, core: 2. Of those that a mesh axis runs over, the one named last changes fastest.
Arguments:
- tokens: bfloat16 [65536, 2048], P(('dp', 'seq', 'head')), parts along dimension 0, may hold values from -6 to 6
- qkv_weight: bfloat16 [2048, 3, 2048], P(None, None, 'head'), may hold values from -0.125 to 0.125
- out_weight: bfloat16 [2048, 2048], P('head'), may hold values from -0.125 to 0.125
- prefix_state: float32 [32, 128, 128], P(('dp', 'head')), parts along dimension 0, may hold values from -1536 to 1536
Outputs:
- layer_out: bfloat16 [65536, 2048], P(('dp', 'seq', 'head')), parts along dimension 0
The draws below stay inside these ranges and needn't reach their ends.
There are 2 independent parts, one for each index of `dp`. The reference program is written for one: setup_inputs(seed, part) draws one part's arguments, and reference() takes and returns one part's arrays. A program takes and returns all parts, laid end to end along the dimension named above; an argument that names none is the same for every part. Nothing has to cross between parts.
All inputs are finite; a program needn't handle non-finite values.
Results may differ from the reference program's by a relative error of at most 0.014.
Values may be sent and summed in bfloat16 or wider, within the bound.
A program may use at most 64 MiB of HBM per device.

```python
import jax
import jax.numpy as jnp
from jax import lax

D = 2048
H = 16
HD = 128
SEQ_DEV = 1024
WINDOW = 32768
N_SEQ = 32
N_HEAD = 4


def steps_of(stream_key, dims, shards, least, largest):
    level = 1.0
    for dim, blocks in shards:
        heights = jax.random.uniform(jax.random.fold_in(jax.random.fold_in(stream_key, 6), dim), (blocks,), jnp.float32, least / len(shards), largest / len(shards))
        level = level * jnp.repeat(jnp.exp(heights), dims[dim] // blocks).reshape((-1,) + (1,) * (len(dims) - 1 - dim))
    return level


def normal_values(stream_key, shape, scale, reach, split=(), held_as=jnp.bfloat16):
    result = scale * jax.random.normal(stream_key, shape, jnp.float32)
    if split:
        result = result * steps_of(stream_key, shape, split, -0.22, 0.18)
    return jnp.clip(result, -reach, reach).astype(held_as)


def setup_inputs(seed: int = 0, part: int = 0) -> dict:
    key_of = jax.random.split(jax.random.key(seed), 5)
    own_keys = jax.random.split(jax.random.fold_in(key_of[4], part), 5)
    return {
        "tokens": normal_values(own_keys[0], (WINDOW, D), 1.0, 6.0, ((0, 128),)),
        "qkv_weight": normal_values(key_of[1], (D, 3, D), D ** -0.5, 0.125, ((2, 4),)),
        "out_weight": normal_values(key_of[2], (D, D), D ** -0.5, 0.125, ((0, 4),)),
        "prefix_state": normal_values(own_keys[3], (H, HD, HD), (WINDOW // 128 + 8), 1536.0, ((0, 4),), jnp.float32),
    }


def reference(tokens, qkv_weight, out_weight, prefix_state):
    total_rows = tokens.shape[0]
    highest = lax.Precision.HIGHEST
    flat = qkv_weight.reshape(D, 3 * D)
    projected = jnp.dot(tokens, flat, preferred_element_type=jnp.float32).astype(jnp.bfloat16)
    projected = projected.reshape(N_SEQ, SEQ_DEV, 3, H, HD).astype(jnp.float32)
    query = projected[:, :, 0]
    keys = projected[:, :, 1]
    values = projected[:, :, 2]

    def state_of(pair):
        return jnp.einsum('thd,the->hde', pair[0], pair[1], precision=highest)
    states = lax.map(state_of, (keys, values))
    earlier = jnp.concatenate([jnp.zeros_like(states[:1]), jnp.cumsum(states, axis=0)[:-1]], axis=0)
    carried = (prefix_state[None] + earlier).astype(jnp.bfloat16).astype(jnp.float32)
    positions = jnp.arange(SEQ_DEV)
    causal = positions[:, None] >= positions[None, :]

    def block_out(items):
        block_q, block_k, block_v, block_c = items
        scores = jnp.einsum('shd,thd->hst', block_q, block_k, precision=highest)
        weights = jnp.where(causal[None], scores, 0.0).astype(jnp.bfloat16).astype(jnp.float32)
        mixed = jnp.einsum('hst,thd->shd', weights, block_v, precision=highest)
        mixed = mixed + jnp.einsum('shd,hde->she', block_q, block_c, precision=highest)
        factor = lax.rsqrt(lax.optimization_barrier(jnp.mean(mixed * mixed, axis=-1, keepdims=True)) + 1e-06)
        return (mixed * factor).astype(jnp.bfloat16)
    normed = lax.map(block_out, (query, keys, values, carried)).reshape(total_rows, D)
    group_width = D // N_HEAD
    summed = jnp.zeros((total_rows, D), jnp.float32)
    for group in range(N_HEAD):
        lower = group * group_width
        upper = lower + group_width
        partial_sum = jnp.dot(normed[:, lower:upper], out_weight[lower:upper], preferred_element_type=jnp.float32)
        summed = summed + partial_sum.astype(jnp.bfloat16).astype(jnp.float32)
    return (tokens.astype(jnp.float32) + summed).astype(jnp.bfloat16)
```

```python
import functools

import jax
import jax.numpy as jnp
from jax import lax
from jax.experimental import pallas as pl
from jax.experimental.pallas import tpu as pltpu
from jax.sharding import PartitionSpec as P

MESH = pl.DeviceIdType.MESH
F32 = jnp.float32
BF16 = jnp.bfloat16

NZ = 8
NX = 4
PIECES = 4
HALVES = 2


class Ring:
    def __init__(self, block, me, n, sgn, device, send, recv, pieces=1):
        self.block, self.me, self.n, self.sgn = block, me, n, sgn
        self.device, self.send, self.recv = device, send, recv
        self.pieces = pieces
        self.far = n // 2
        self.near = n - 1 - self.far

    def at(self, steps):
        return lax.rem(self.me + self.sgn * steps + 2 * self.n, self.n)

    def hops(self, way):
        return self.far if way > 0 else self.near

    def sem(self, way, hop, piece):
        base = 0 if way > 0 else self.far
        return (base + hop) * self.pieces + piece

    def copy(self, way, hop, piece, src, dst):
        number = self.sem(way, hop, piece)
        return pltpu.make_async_remote_copy(
            src_ref=src,
            dst_ref=dst,
            send_sem=self.send.at[number],
            recv_sem=self.recv.at[number],
            device_id=self.device(self.at(way)),
            device_id_type=MESH,
        )

    def start(self, way, hop, piece=0, src=None):
        if hop < self.hops(way):
            here = self.block(-way * hop, self.at(-way * hop), piece)
            self.copy(way, hop, piece, here if src is None else src, self.landing(way, hop, piece)).start()

    def landing(self, way, hop, piece):
        return self.block(-way * (hop + 1), self.at(-way * hop), piece)

    def arrived(self, way, hop, piece=0):
        if hop < self.hops(way):
            here = self.block(-way * (hop + 1), self.at(-way * (hop + 1)), piece)
            self.copy(way, hop, piece, here, here).wait_recv()

    def pass_on(self, way, hop, piece=0):
        self.arrived(way, hop, piece)
        self.start(way, hop + 1, piece)

    def finish(self):
        for way in (1, -1):
            for hop in range(self.hops(way)):
                for piece in range(self.pieces):
                    here = self.block(-way * hop, self.at(-way * hop), piece)
                    self.copy(way, hop, piece, here, here).wait_send()


def kernel(
    ny,
    tok_hbm,
    wq_hbm,
    wo_hbm,
    prefix_ref,
    out_ref,
    tok,
    wq,
    wo,
    qkv,
    st,
    off,
    mixed,
    nbuf,
    nrec,
    acc,
    sbuf,
    rbuf,
    pbuf,
    cbuf,
    lsem,
    tsend,
    trecv,
    xsend,
    xrecv,
    r1send,
    r1recv,
    r2send,
    r2recv,
    bsend,
    brecv,
    ssend,
    srecv,
    csend,
    crecv,
    nsend,
    nrecv,
):
    nseq = ny * NZ
    rows = tok.shape[1]
    heads = st.shape[1]
    hd = st.shape[2]
    width = wo.shape[-1]
    me = lax.axis_index("seq")
    mx = lax.axis_index("head")
    mc = lax.axis_index("dp")
    my = me // NZ
    mz = lax.rem(me, NZ)
    sgn = 1 - 2 * mc

    loads = [pltpu.make_async_copy(tok_hbm, tok.at[0], lsem.at[0])]
    for part in range(3):
        loads.append(pltpu.make_async_copy(wq_hbm.at[part], wq.at[part], lsem.at[1 + part]))
    for band in range(4):
        loads.append(
            pltpu.make_async_copy(
                wo_hbm.at[:, :, :, pl.ds(band * width, width)], wo.at[band, 0], lsem.at[4 + band]
            )
        )
    for load in loads:
        load.start()

    barrier = pltpu.get_barrier_semaphore()
    for step in range(1, NX):
        pl.semaphore_signal(
            barrier, inc=1, device_id={"head": lax.rem(mx + step, NX)}, device_id_type=MESH
        )
    pl.semaphore_signal(barrier, inc=1, device_id={"dp": 1 - mc}, device_id_type=MESH)

    def greet(step, carry):
        pl.semaphore_signal(
            barrier, inc=1, device_id={"seq": lax.rem(me + step, nseq)}, device_id_type=MESH
        )
        return carry

    lax.fori_loop(1, nseq, greet, 0)
    pl.semaphore_wait(barrier, NX - 1 + 1 + nseq - 1)

    def slice_copy(side, step):
        band = mc * 2 + side
        number = side * (NX - 1) + step - 1
        return pltpu.make_async_remote_copy(
            src_ref=wo_hbm.at[my, mz, :, pl.ds(pl.multiple_of(band * width, width), width)],
            dst_ref=wo.at[band, NX - step, my, mz],
            send_sem=xsend.at[number],
            recv_sem=xrecv.at[number],
            device_id={"head": lax.rem(mx + step, NX)},
            device_id_type=MESH,
        )

    for side in range(2):
        for step in range(1, NX):
            slice_copy(side, step).start()

    prow = rows // PIECES

    def tok_block(relative, index, piece):
        return tok.at[relative % NX, pl.ds(piece * prow, prow)]

    tring = Ring(
        tok_block, mx, NX, sgn, lambda index: {"head": index}, tsend, trecv, pieces=PIECES
    )
    for piece in range(PIECES):
        for way in (1, -1):
            tring.start(way, 0, piece, src=tok_hbm.at[pl.ds(piece * prow, prow)])

    def along_y(index):
        return {"seq": index * NZ + mz}

    def along_z(index):
        return {"seq": my * NZ + index}

    first = [
        Ring(
            lambda relative, index, piece: wo.at[mc * 2, pl.ds(1, NX - 1), index, mz],
            my, ny, sgn, along_y, r1send.at[0], r1recv.at[0],
        ),
        Ring(
            lambda relative, index, piece: wo.at[mc * 2 + 1, pl.ds(1, NX - 1), my, index],
            mz, NZ, sgn, along_z, r1send.at[1], r1recv.at[1],
        ),
    ]
    second = [
        Ring(
            lambda relative, index, piece: wo.at[mc * 2, pl.ds(1, NX - 1), :, index],
            mz, NZ, sgn, along_z, r2send.at[0], r2recv.at[0],
        ),
        Ring(
            lambda relative, index, piece: wo.at[mc * 2 + 1, pl.ds(1, NX - 1), index],
            my, ny, sgn, along_y, r2send.at[1], r2recv.at[1],
        ),
    ]

    def hop(ring, number):
        for way in (1, -1):
            ring.pass_on(way, number)

    def begin(ring):
        for way in (1, -1):
            ring.start(way, 0)

    def group_of(slot):
        return lax.rem(mx + sgn * slot + 2 * NX, NX)

    def project(slot, lower, count):
        group = group_of(slot)
        pair = wq.shape[2] // 2

        def body(step, carry):
            part = step // 2
            side = lax.rem(step, 2)
            result = jnp.dot(
                tok[slot, pl.ds(lower, count)],
                wq[part, :, pl.ds(pl.multiple_of(side * pair, pair), pair)],
                preferred_element_type=F32,
            ).astype(BF16)
            for half in range(2):
                qkv[part * heads + side * 2 + half, group, pl.ds(lower, count)] = result[
                    :, half * hd : (half + 1) * hd
                ]
            return carry

        lax.fori_loop(0, 6, body, 0)

    def state(slot):
        group = group_of(slot)
        for head in range(heads):
            st[group, head] = lax.dot_general(
                qkv[heads + head, group],
                qkv[2 * heads + head, group],
                (((0,), (0,)), ((), ())),
                preferred_element_type=F32,
            )

    def slices_in(side):
        for step in range(1, NX):
            copy = slice_copy(side, step)
            band = mc * 2 + side
            number = side * (NX - 1) + step - 1
            here = wo.at[band, NX - step, my, mz]
            pltpu.make_async_remote_copy(
                src_ref=here, dst_ref=here, send_sem=xsend.at[number], recv_sem=xrecv.at[number],
                device_id={"head": lax.rem(mx + step, NX)}, device_id_type=MESH,
            ).wait_recv()
        begin(first[side])

    for side in range(2):
        slices_in(side)
    for load in loads[:4]:
        load.wait()
    project(0, 0, rows)
    hop(first[0], 0)
    hop(first[1], 0)
    hop(first[0], 1)
    begin(second[0])
    hop(first[1], 1)
    tring.pass_on(1, 0, 0)
    hop(first[1], 2)
    hop(first[1], 3)
    begin(second[1])
    state(0)
    tring.pass_on(1, 0, 1)
    hop(second[0], 0)
    tring.pass_on(1, 0, 2)
    tring.pass_on(1, 0, 3)
    hop(second[0], 1)
    hop(second[1], 0)
    project(NX - 1, 0, rows)
    state(NX - 1)
    for piece in range(PIECES):
        tring.arrived(-1, 0, piece)
    project(1, 0, rows)
    state(1)
    hop(second[0], 2)
    hop(second[0], 3)
    hop(second[1], 1)

    def sibling(side):
        band = wo.at[mc * 2 + side, pl.ds(1, NX - 1)]
        return pltpu.make_async_remote_copy(
            src_ref=band, dst_ref=band, send_sem=bsend.at[side], recv_sem=brecv.at[side],
            device_id={"dp": 1 - mc}, device_id_type=MESH,
        )

    for side in range(2):
        sibling(side).start()

    for half in range(2):
        for piece in range(half * PIECES // 2, (half + 1) * PIECES // 2):
            tring.arrived(1, 1, piece)
        project(2, half * rows // 2, rows // 2)
    state(2)

    per_head = nseq // heads
    for head in range(heads):
        total = st[0, head] + st[1, head] + st[2, head] + st[3, head]
        sbuf[head * per_head : (head + 1) * per_head] = total.astype(BF16).reshape(
            per_head, hd // per_head, hd
        )

    def out_copy(step):
        to = lax.rem(me + step, nseq)
        return pltpu.make_async_remote_copy(
            src_ref=sbuf.at[to], dst_ref=rbuf.at[me], send_sem=ssend.at[step],
            recv_sem=srecv.at[step], device_id={"seq": to}, device_id_type=MESH,
        )

    def in_copy(step):
        here = lax.rem(me - step + nseq, nseq)
        return pltpu.make_async_remote_copy(
            src_ref=sbuf.at[here], dst_ref=rbuf.at[here], send_sem=ssend.at[step],
            recv_sem=srecv.at[step], device_id={"seq": here}, device_id_type=MESH,
        )

    def back_copy(step):
        to = lax.rem(me + step, nseq)
        return pltpu.make_async_remote_copy(
            src_ref=pbuf.at[to], dst_ref=cbuf.at[me], send_sem=csend.at[step],
            recv_sem=crecv.at[step], device_id={"seq": to}, device_id_type=MESH,
        )

    def carried_copy(step):
        here = lax.rem(me - step + nseq, nseq)
        return pltpu.make_async_remote_copy(
            src_ref=pbuf.at[here], dst_ref=cbuf.at[here], send_sem=csend.at[step],
            recv_sem=crecv.at[step], device_id={"seq": here}, device_id_type=MESH,
        )

    def each(action):
        def body(step, carry):
            action(step)
            return carry

        lax.fori_loop(1, nseq, body, 0)

    each(lambda step: out_copy(step).start())
    rbuf[me] = sbuf[me]

    for head in range(heads):
        running = st[0, head]
        off[1, head] = running.astype(BF16)
        for group in range(2, NX):
            running = running + st[group - 1, head]
            off[group, head] = running.astype(BF16)
        off[0, head] = jnp.zeros((hd, hd), BF16)

    def inner(group):
        causal = lax.broadcasted_iota(jnp.int32, (rows, rows), 0) >= lax.broadcasted_iota(
            jnp.int32, (rows, rows), 1
        )
        for head in range(heads):
            query = qkv[head, group]
            scores = lax.dot_general(
                query, qkv[heads + head, group], (((1,), (1,)), ((), ())),
                preferred_element_type=F32,
            )
            weights = jnp.where(causal, scores, 0.0).astype(BF16)
            mixed[group, head] = jnp.dot(
                weights, qkv[2 * heads + head, group], preferred_element_type=F32
            ) + jnp.dot(query, off[group, head], preferred_element_type=F32)

    def inner_body(group, carry):
        inner(group)
        return carry

    lax.fori_loop(0, 1, inner_body, 0)

    each(lambda step: in_copy(step).wait_recv())
    total = prefix_ref[me]
    for block in range(nseq):
        pbuf[block] = total.astype(BF16)
        if block < nseq - 1:
            total = total + rbuf[block].astype(F32)
    each(lambda step: back_copy(step).start())
    cbuf[me] = pbuf[me]

    lax.fori_loop(1, NX, inner_body, 0)
    each(lambda step: carried_copy(step).wait_recv())

    hrow = rows // HALVES

    def normed_copy(step, half):
        number = (step - 1) * HALVES + half
        return pltpu.make_async_remote_copy(
            src_ref=nbuf.at[step, pl.ds(half * hrow, hrow)],
            dst_ref=nrec.at[NX - step - 1, pl.ds(half * hrow, hrow)],
            send_sem=nsend.at[number],
            recv_sem=nrecv.at[number],
            device_id={"head": lax.rem(mx + step, NX)},
            device_id_type=MESH,
        )

    def normed_in(step, half):
        number = (NX - step - 1) * HALVES + half
        here = nrec.at[step - 1, pl.ds(half * hrow, hrow)]
        return pltpu.make_async_remote_copy(
            src_ref=here, dst_ref=here, send_sem=nsend.at[number], recv_sem=nrecv.at[number],
            device_id={"head": lax.rem(mx + step, NX)}, device_id_type=MESH,
        )

    def normalize(step, half):
        group = lax.rem(mx + step, NX)
        lower = half * hrow
        for head in range(heads):
            carried = cbuf[head * per_head : (head + 1) * per_head].reshape(hd, hd)
            value = mixed[group, head, pl.ds(lower, hrow)] + jnp.dot(
                qkv[head, group, pl.ds(lower, hrow)], carried, preferred_element_type=F32
            )
            factor = lax.rsqrt(jnp.mean(value * value, axis=-1, keepdims=True) + 1e-06)
            nbuf[step, pl.ds(lower, hrow), head * hd : (head + 1) * hd] = (value * factor).astype(BF16)

    for half in range(HALVES):
        for step in (2, 1, 3):
            normalize(step, half)
            normed_copy(step, half).start()
    for half in range(HALVES):
        normalize(0, half)

    for load in loads[4:]:
        load.wait()

    def weight(band, relative):
        return wo[band, relative].reshape(nseq * 16, width)

    def own(band, carry):
        columns = pl.ds(pl.multiple_of(band * width, width), width)
        acc[:, columns] = tok[0, :, columns].astype(F32) + jnp.dot(
            nbuf[0], weight(band, 0), preferred_element_type=F32
        )
        return carry

    lax.fori_loop(0, 4, own, 0)
    for side in range(2):
        band = wo.at[(1 - mc) * 2 + side, pl.ds(1, NX - 1)]
        pltpu.make_async_remote_copy(
            src_ref=band, dst_ref=band, send_sem=bsend.at[side], recv_sem=brecv.at[side],
            device_id={"dp": 1 - mc}, device_id_type=MESH,
        ).wait_recv()

    for half in range(HALVES):
        lower = half * hrow
        for place, step in enumerate((2, 1, 3)):
            normed_in(step, half).wait_recv()

            def project_out(band, carry):
                columns = pl.ds(pl.multiple_of(band * width, width), width)
                value = acc[lower : lower + hrow, columns] + jnp.dot(
                    nrec[step - 1, lower : lower + hrow], weight(band, step), preferred_element_type=F32
                )
                if place < 2:
                    acc[lower : lower + hrow, columns] = value
                else:
                    out_ref[lower : lower + hrow, columns] = value.astype(BF16)
                return carry

            lax.fori_loop(0, 4, project_out, 0)

    for side in range(2):
        for step in range(1, NX):
            slice_copy(side, step).wait_send()
        sibling(side).wait_send()
    for ring in [tring] + first + second:
        ring.finish()
    each(lambda step: out_copy(step).wait_send())
    each(lambda step: back_copy(step).wait_send())
    for step in range(1, NX):
        for half in range(HALVES):
            normed_copy(step, half).wait_send()


def on_device(tokens, qkv_weight, out_weight, prefix_state):
    rows, model_width = tokens.shape
    heads, hd, _ = prefix_state.shape
    group_width = heads * hd
    nseq = lax.axis_size("seq")
    ny = nseq // NZ
    width = model_width // 4
    slice_rows = group_width // nseq
    dma = pltpu.SemaphoreType.DMA
    return pl.pallas_call(
        functools.partial(kernel, ny),
        out_shape=jax.ShapeDtypeStruct((rows, model_width), BF16),
        in_specs=[pl.BlockSpec(memory_space=pl.ANY)] * 3 + [pl.BlockSpec(memory_space=pltpu.VMEM)],
        out_specs=pl.BlockSpec(memory_space=pltpu.VMEM),
        scratch_shapes=[
            pltpu.VMEM((NX, rows, model_width), BF16),
            pltpu.VMEM((3, model_width, group_width), BF16),
            pltpu.VMEM((4, NX, ny, NZ, slice_rows, width), BF16),
            pltpu.VMEM((3 * heads, NX, rows, hd), BF16),
            pltpu.VMEM((NX, heads, hd, hd), F32),
            pltpu.VMEM((NX, heads, hd, hd), BF16),
            pltpu.VMEM((NX, heads, rows, hd), F32),
            pltpu.VMEM((NX, rows, group_width), BF16),
            pltpu.VMEM((NX - 1, rows, group_width), BF16),
            pltpu.VMEM((rows, model_width), F32),
            pltpu.VMEM((nseq, slice_rows, hd), BF16),
            pltpu.VMEM((nseq, slice_rows, hd), BF16),
            pltpu.VMEM((nseq, slice_rows, hd), BF16),
            pltpu.VMEM((nseq, slice_rows, hd), BF16),
            dma((8,)),
            dma((3 * PIECES,)),
            dma((3 * PIECES,)),
            dma((2 * (NX - 1),)),
            dma((2 * (NX - 1),)),
            dma((2, NZ)),
            dma((2, NZ)),
            dma((2, NZ)),
            dma((2, NZ)),
            dma((2,)),
            dma((2,)),
            dma((nseq,)),
            dma((nseq,)),
            dma((nseq,)),
            dma((nseq,)),
            dma(((NX - 1) * HALVES,)),
            dma(((NX - 1) * HALVES,)),
        ],
        compiler_params=pltpu.CompilerParams(
            collective_id=0, has_side_effects=True, vmem_limit_bytes=56 * 1024 * 1024
        ),
        name="layer",
    )(
        tokens,
        jnp.transpose(qkv_weight, (1, 0, 2)),
        out_weight.reshape(ny, NZ, slice_rows, model_width),
        prefix_state.reshape(nseq, slice_rows, hd),
    )


def solution(mesh):
    return jax.shard_map(
        on_device,
        mesh=mesh,
        in_specs=(
            P(("dp", "seq", "head"), None),
            P(None, None, "head"),
            P("head", None),
            P(("dp", "head"), None, None),
        ),
        out_specs=P(("dp", "seq", "head"), None),
        check_vma=False,
    )
```

```python
import functools

import jax
import jax.numpy as jnp
from jax import lax
from jax.experimental import pallas as pl
from jax.experimental.pallas import tpu as pltpu
from jax.sharding import PartitionSpec as P

MESH = pl.DeviceIdType.MESH
F32 = jnp.float32
BF16 = jnp.bfloat16

NZ = 8
NX = 4
PIECES = 4
HALVES = 2


class Ring:
    def __init__(self, block, me, n, sgn, device, send, recv, pieces=1):
        self.block, self.me, self.n, self.sgn = block, me, n, sgn
        self.device, self.send, self.recv = device, send, recv
        self.pieces = pieces
        self.far = n // 2
        self.near = n - 1 - self.far

    def at(self, steps):
        return lax.rem(self.me + self.sgn * steps + 2 * self.n, self.n)

    def hops(self, way):
        return self.far if way > 0 else self.near

    def sem(self, way, hop, piece):
        base = 0 if way > 0 else self.far
        return (base + hop) * self.pieces + piece

    def copy(self, way, hop, piece, src, dst):
        number = self.sem(way, hop, piece)
        return pltpu.make_async_remote_copy(
            src_ref=src,
            dst_ref=dst,
            send_sem=self.send.at[number],
            recv_sem=self.recv.at[number],
            device_id=self.device(self.at(way)),
            device_id_type=MESH,
        )

    def start(self, way, hop, piece=0, src=None):
        if hop < self.hops(way):
            here = self.block(-way * hop, self.at(-way * hop), piece)
            self.copy(way, hop, piece, here if src is None else src, self.landing(way, hop, piece)).start()

    def landing(self, way, hop, piece):
        return self.block(-way * (hop + 1), self.at(-way * hop), piece)

    def arrived(self, way, hop, piece=0):
        if hop < self.hops(way):
            here = self.block(-way * (hop + 1), self.at(-way * (hop + 1)), piece)
            self.copy(way, hop, piece, here, here).wait_recv()

    def pass_on(self, way, hop, piece=0):
        self.arrived(way, hop, piece)
        self.start(way, hop + 1, piece)

    def finish(self):
        for way in (1, -1):
            for hop in range(self.hops(way)):
                for piece in range(self.pieces):
                    here = self.block(-way * hop, self.at(-way * hop), piece)
                    self.copy(way, hop, piece, here, here).wait_send()


def kernel(
    ny,
    tok_hbm,
    wq_hbm,
    wo_hbm,
    prefix_hbm,
    out_hbm,
    tok,
    wq,
    wo,
    qkv,
    st,
    off,
    mixed,
    nbuf,
    nrec,
    acc,
    sbuf,
    rbuf,
    pbuf,
    cbuf,
    prefix,
    out,
    lsem,
    osem,
    tsend,
    trecv,
    xsend,
    xrecv,
    r1send,
    r1recv,
    r2send,
    r2recv,
    bsend,
    brecv,
    ssend,
    srecv,
    csend,
    crecv,
    nsend,
    nrecv,
):
    nseq = ny * NZ
    rows = tok.shape[1]
    heads = st.shape[1]
    hd = st.shape[2]
    width = wo.shape[-1]
    me = lax.axis_index("seq")
    mx = lax.axis_index("head")
    mc = lax.axis_index("dp")
    my = me // NZ
    mz = lax.rem(me, NZ)
    sgn = 1 - 2 * mc

    barrier = pltpu.get_barrier_semaphore()
    for step in range(1, NX):
        pl.semaphore_signal(
            barrier, inc=1, device_id={"head": lax.rem(mx + step, NX)}, device_id_type=MESH
        )
    pl.semaphore_signal(barrier, inc=1, device_id={"dp": 1 - mc}, device_id_type=MESH)

    for step in (1, NZ - 1):
        pl.semaphore_signal(
            barrier, inc=1, device_id={"seq": my * NZ + lax.rem(mz + step, NZ)}, device_id_type=MESH
        )
    for step in (1, ny - 1):
        pl.semaphore_signal(
            barrier, inc=1, device_id={"seq": lax.rem(my + step, ny) * NZ + mz}, device_id_type=MESH
        )
    loads = [pltpu.make_async_copy(tok_hbm, tok.at[0], lsem.at[0])]
    for part in range(3):
        loads.append(pltpu.make_async_copy(wq_hbm.at[part], wq.at[part], lsem.at[1 + part]))
    for band in range(4):
        loads.append(
            pltpu.make_async_copy(
                wo_hbm.at[:, :, :, pl.ds(band * width, width)], wo.at[band, 0], lsem.at[4 + band]
            )
        )
    loads.append(pltpu.make_async_copy(prefix_hbm.at[me], prefix, lsem.at[8]))
    for load in loads:
        load.start()

    pl.semaphore_wait(barrier, NX - 1 + 1 + 4)

    def slice_copy(side, step):
        band = mc * 2 + side
        number = side * (NX - 1) + step - 1
        return pltpu.make_async_remote_copy(
            src_ref=wo_hbm.at[my, mz, :, pl.ds(pl.multiple_of(band * width, width), width)],
            dst_ref=wo.at[band, NX - step, my, mz],
            send_sem=xsend.at[number],
            recv_sem=xrecv.at[number],
            device_id={"head": lax.rem(mx + step, NX)},
            device_id_type=MESH,
        )

    for side in range(2):
        for step in range(1, NX):
            slice_copy(side, step).start()

    prow = rows // PIECES

    loads[0].wait()

    def tok_copy(way, hop, piece, slot, landing):
        number = ((0 if way > 0 else 1) + 2 * hop) * PIECES + piece
        lower = piece * prow
        return pltpu.make_async_remote_copy(
            src_ref=tok.at[slot, pl.ds(lower, prow)],
            dst_ref=tok.at[landing, pl.ds(lower, prow)],
            send_sem=tsend.at[number],
            recv_sem=trecv.at[number],
            device_id={"head": lax.rem(mx + way + NX, NX)},
            device_id_type=MESH,
        )

    side_of = {1: NX - 1, -1: 1}
    middle = PIECES // 2
    passed = {1: range(middle), -1: range(middle, PIECES)}

    def tok_start(way, hop, piece):
        if hop == 0:
            tok_copy(way, 0, piece, 0, side_of[way]).start()
        else:
            tok_copy(way, 1, piece, side_of[way], 2).start()

    def tok_arrived(way, hop, piece):
        here = side_of[way] if hop == 0 else 2
        tok_copy(way, hop, piece, here, here).wait_recv()

    for step in range(PIECES):
        tok_start(1, 0, step)
        tok_start(-1, 0, (step + middle) % PIECES)

    def along_y(index):
        return {"seq": index * NZ + mz}

    def along_z(index):
        return {"seq": my * NZ + index}

    first = [
        Ring(
            lambda relative, index, piece: wo.at[mc * 2, pl.ds(1, NX - 1), index, mz],
            my, ny, sgn, along_y, r1send.at[0], r1recv.at[0],
        ),
        Ring(
            lambda relative, index, piece: wo.at[mc * 2 + 1, pl.ds(1, NX - 1), my, index],
            mz, NZ, sgn, along_z, r1send.at[1], r1recv.at[1],
        ),
    ]
    second = [
        Ring(
            lambda relative, index, piece: wo.at[mc * 2, pl.ds(1, NX - 1), :, index],
            mz, NZ, sgn, along_z, r2send.at[0], r2recv.at[0],
        ),
        Ring(
            lambda relative, index, piece: wo.at[mc * 2 + 1, pl.ds(1, NX - 1), index],
            my, ny, sgn, along_y, r2send.at[1], r2recv.at[1],
        ),
    ]

    def hop(ring, number):
        for way in (1, -1):
            ring.pass_on(way, number)

    def begin(ring):
        for way in (1, -1):
            ring.start(way, 0)

    def group_of(slot):
        return lax.rem(mx + slot, NX)

    def project(slot, first_part=0, parts=3, lower=0, count=rows):
        group = group_of(slot)
        pair = wq.shape[2] // 2

        def body(step, carry):
            part = step // 2
            side = lax.rem(step, 2)
            result = jnp.dot(
                tok[slot, pl.ds(lower, count)],
                wq[part, :, pl.ds(pl.multiple_of(side * pair, pair), pair)],
                preferred_element_type=F32,
            ).astype(BF16)
            for half in range(2):
                qkv[part * heads + side * 2 + half, group, pl.ds(lower, count)] = result[
                    :, half * hd : (half + 1) * hd
                ]
            return carry

        lax.fori_loop(2 * first_part, 2 * (first_part + parts), body, 0)

    def state(slot):
        group = group_of(slot)
        for head in range(heads):
            st[group, head] = lax.dot_general(
                qkv[heads + head, group],
                qkv[2 * heads + head, group],
                (((0,), (0,)), ((), ())),
                preferred_element_type=F32,
            )

    def slices_in(side):
        for step in range(1, NX):
            band = mc * 2 + side
            number = side * (NX - 1) + step - 1
            here = wo.at[band, NX - step, my, mz]
            pltpu.make_async_remote_copy(
                src_ref=here, dst_ref=here, send_sem=xsend.at[number], recv_sem=xrecv.at[number],
                device_id={"head": lax.rem(mx + step, NX)}, device_id_type=MESH,
            ).wait_recv()
        begin(first[side])

    for side in range(2):
        slices_in(side)
    for load in loads[1:4]:
        load.wait()
    project(0)
    hop(first[0], 0)
    hop(first[1], 0)
    hop(first[0], 1)
    begin(second[0])
    hop(first[1], 1)
    hop(first[1], 2)
    state(0)
    hop(first[1], 3)
    begin(second[1])
    hop(second[0], 0)
    for step in range(middle):
        for way in (1, -1):
            piece = passed[way][step]
            tok_arrived(way, 0, piece)
            tok_start(way, 1, piece)
    hop(second[0], 1)
    hop(second[1], 0)
    for way in (1, -1):
        for piece in passed[-way]:
            tok_arrived(way, 0, piece)
        project(side_of[way])
        state(side_of[way])
    hop(second[0], 2)

    def sibling(side):
        band = wo.at[mc * 2 + side, pl.ds(1, NX - 1)]
        return pltpu.make_async_remote_copy(
            src_ref=band, dst_ref=band, send_sem=bsend.at[side], recv_sem=brecv.at[side],
            device_id={"dp": 1 - mc}, device_id_type=MESH,
        )

    for way in (1, -1):
        for piece in passed[way]:
            tok_arrived(way, 1, piece)
    project(2, 1, 2)
    state(2)

    per_head = nseq // heads
    for head in range(heads):
        total = st[0, head] + st[1, head] + st[2, head] + st[3, head]
        sbuf[head * per_head : (head + 1) * per_head] = total.astype(BF16).reshape(
            per_head, hd // per_head, hd
        )

    def out_copy(step):
        to = lax.rem(me + step, nseq)
        return pltpu.make_async_remote_copy(
            src_ref=sbuf.at[to], dst_ref=rbuf.at[me], send_sem=ssend.at[step],
            recv_sem=srecv.at[step], device_id={"seq": to}, device_id_type=MESH,
        )

    def in_copy(step):
        here = lax.rem(me - step + nseq, nseq)
        return pltpu.make_async_remote_copy(
            src_ref=sbuf.at[here], dst_ref=rbuf.at[here], send_sem=ssend.at[step],
            recv_sem=srecv.at[step], device_id={"seq": here}, device_id_type=MESH,
        )

    def back_copy(step):
        to = lax.rem(me + step, nseq)
        return pltpu.make_async_remote_copy(
            src_ref=pbuf.at[to], dst_ref=cbuf.at[me], send_sem=csend.at[step],
            recv_sem=crecv.at[step], device_id={"seq": to}, device_id_type=MESH,
        )

    def carried_copy(step):
        here = lax.rem(me - step + nseq, nseq)
        return pltpu.make_async_remote_copy(
            src_ref=pbuf.at[here], dst_ref=cbuf.at[here], send_sem=csend.at[step],
            recv_sem=crecv.at[step], device_id={"seq": here}, device_id_type=MESH,
        )

    def each(action):
        def body(step, carry):
            action(step)
            return carry

        lax.fori_loop(1, nseq, body, 0)

    def hops_to(step):
        around_z, around_y = step % NZ, step // NZ
        return min(around_z, NZ - around_z) + min(around_y, ny - around_y)

    def far_first(action):
        for step in sorted(range(1, nseq), key=hops_to, reverse=True):
            action(step)

    far_first(lambda step: out_copy(step).start())
    rbuf[me] = sbuf[me]
    project(2, 0, 1)

    for head in range(heads):
        running = st[0, head]
        off[1, head] = running.astype(BF16)
        for group in range(2, NX):
            running = running + st[group - 1, head]
            off[group, head] = running.astype(BF16)
        off[0, head] = jnp.zeros((hd, hd), BF16)

    def inner(group):
        causal = lax.broadcasted_iota(jnp.int32, (rows, rows), 0) >= lax.broadcasted_iota(
            jnp.int32, (rows, rows), 1
        )
        for head in range(heads):
            query = qkv[head, group]
            scores = lax.dot_general(
                query, qkv[heads + head, group], (((1,), (1,)), ((), ())),
                preferred_element_type=F32,
            )
            weights = jnp.where(causal, scores, 0.0).astype(BF16)
            mixed[group, head] = jnp.dot(
                weights, qkv[2 * heads + head, group], preferred_element_type=F32
            ) + jnp.dot(query, off[group, head], preferred_element_type=F32)

    def inner_body(group, carry):
        inner(group)
        return carry

    lax.fori_loop(0, 1, inner_body, 0)

    each(lambda step: in_copy(step).wait_recv())
    loads[8].wait()
    total = prefix[...]
    for block in range(nseq):
        pbuf[block] = total.astype(BF16)
        if block < nseq - 1:
            total = total + rbuf[block].astype(F32)
    far_first(lambda step: back_copy(step).start())
    cbuf[me] = pbuf[me]
    hop(second[0], 3)
    hop(second[1], 1)
    for side in range(2):
        sibling(side).start()

    lax.fori_loop(1, NX, inner_body, 0)
    each(lambda step: carried_copy(step).wait_recv())

    hrow = rows // HALVES

    def normed_copy(step, half):
        number = (step - 1) * HALVES + half
        return pltpu.make_async_remote_copy(
            src_ref=nbuf.at[step, pl.ds(half * hrow, hrow)],
            dst_ref=nrec.at[NX - step - 1, pl.ds(half * hrow, hrow)],
            send_sem=nsend.at[number],
            recv_sem=nrecv.at[number],
            device_id={"head": lax.rem(mx + step, NX)},
            device_id_type=MESH,
        )

    def normed_in(step, half):
        number = (NX - step - 1) * HALVES + half
        here = nrec.at[step - 1, pl.ds(half * hrow, hrow)]
        return pltpu.make_async_remote_copy(
            src_ref=here, dst_ref=here, send_sem=nsend.at[number], recv_sem=nrecv.at[number],
            device_id={"head": lax.rem(mx + step, NX)}, device_id_type=MESH,
        )

    def normalize(step, half):
        group = lax.rem(mx + step, NX)
        lower = half * hrow
        for head in range(heads):
            carried = cbuf[head * per_head : (head + 1) * per_head].reshape(hd, hd)
            value = mixed[group, head, pl.ds(lower, hrow)] + jnp.dot(
                qkv[head, group, pl.ds(lower, hrow)], carried, preferred_element_type=F32
            )
            factor = lax.rsqrt(jnp.mean(value * value, axis=-1, keepdims=True) + 1e-06)
            nbuf[step, pl.ds(lower, hrow), head * hd : (head + 1) * hd] = (value * factor).astype(BF16)

    for half in range(HALVES):
        for step in (2, 1, 3):
            normalize(step, half)
            normed_copy(step, half).start()
    for half in range(HALVES):
        normalize(0, half)

    for load in loads[4:8]:
        load.wait()

    def weight(band, relative):
        return wo[band, relative].reshape(nseq * 16, width)

    def own(band, carry):
        columns = pl.ds(pl.multiple_of(band * width, width), width)
        acc[:, columns] = tok[0, :, columns].astype(F32) + jnp.dot(
            nbuf[0], weight(band, 0), preferred_element_type=F32
        )
        return carry

    lax.fori_loop(0, 4, own, 0)
    for side in range(2):
        band = wo.at[(1 - mc) * 2 + side, pl.ds(1, NX - 1)]
        pltpu.make_async_remote_copy(
            src_ref=band, dst_ref=band, send_sem=bsend.at[side], recv_sem=brecv.at[side],
            device_id={"dp": 1 - mc}, device_id_type=MESH,
        ).wait_recv()

    def out_store(half):
        part = pl.ds(half * hrow, hrow)
        return pltpu.make_async_copy(out.at[part], out_hbm.at[part], osem.at[half])

    for half in range(HALVES):
        lower = half * hrow
        for place, step in enumerate((2, 1, 3)):
            normed_in(step, half).wait_recv()

            def project_out(band, carry):
                columns = pl.ds(pl.multiple_of(band * width, width), width)
                value = acc[lower : lower + hrow, columns] + jnp.dot(
                    nrec[step - 1, lower : lower + hrow], weight(band, step), preferred_element_type=F32
                )
                if place < 2:
                    acc[lower : lower + hrow, columns] = value
                else:
                    out[lower : lower + hrow, columns] = value.astype(BF16)
                return carry

            lax.fori_loop(0, 4, project_out, 0)
        out_store(half).start()

    for half in range(HALVES):
        out_store(half).wait()
    for side in range(2):
        for step in range(1, NX):
            slice_copy(side, step).wait_send()
        sibling(side).wait_send()
    for ring in first + second:
        ring.finish()
    for way in (1, -1):
        for piece in range(PIECES):
            tok_copy(way, 0, piece, 0, side_of[way]).wait_send()
        for piece in passed[way]:
            tok_copy(way, 1, piece, side_of[way], 2).wait_send()
    each(lambda step: out_copy(step).wait_send())
    each(lambda step: back_copy(step).wait_send())
    for step in range(1, NX):
        for half in range(HALVES):
            normed_copy(step, half).wait_send()


def on_device(tokens, qkv_weight, out_weight, prefix_state):
    rows, model_width = tokens.shape
    heads, hd, _ = prefix_state.shape
    group_width = heads * hd
    nseq = lax.axis_size("seq")
    ny = nseq // NZ
    width = model_width // 4
    slice_rows = group_width // nseq
    dma = pltpu.SemaphoreType.DMA
    return pl.pallas_call(
        functools.partial(kernel, ny),
        out_shape=jax.ShapeDtypeStruct((rows, model_width), BF16),
        in_specs=[pl.BlockSpec(memory_space=pl.ANY)] * 4,
        out_specs=pl.BlockSpec(memory_space=pl.ANY),
        scratch_shapes=[
            pltpu.VMEM((NX, rows, model_width), BF16),
            pltpu.VMEM((3, model_width, group_width), BF16),
            pltpu.VMEM((4, NX, ny, NZ, slice_rows, width), BF16),
            pltpu.VMEM((3 * heads, NX, rows, hd), BF16),
            pltpu.VMEM((NX, heads, hd, hd), F32),
            pltpu.VMEM((NX, heads, hd, hd), BF16),
            pltpu.VMEM((NX, heads, rows, hd), F32),
            pltpu.VMEM((NX, rows, group_width), BF16),
            pltpu.VMEM((NX - 1, rows, group_width), BF16),
            pltpu.VMEM((rows, model_width), F32),
            pltpu.VMEM((nseq, slice_rows, hd), BF16),
            pltpu.VMEM((nseq, slice_rows, hd), BF16),
            pltpu.VMEM((nseq, slice_rows, hd), BF16),
            pltpu.VMEM((nseq, slice_rows, hd), BF16),
            pltpu.VMEM((slice_rows, hd), F32),
            pltpu.VMEM((rows, model_width), BF16),
            dma((9,)),
            dma((HALVES,)),
            dma((4 * PIECES,)),
            dma((4 * PIECES,)),
            dma((2 * (NX - 1),)),
            dma((2 * (NX - 1),)),
            dma((2, NZ)),
            dma((2, NZ)),
            dma((2, NZ)),
            dma((2, NZ)),
            dma((2,)),
            dma((2,)),
            dma((nseq,)),
            dma((nseq,)),
            dma((nseq,)),
            dma((nseq,)),
            dma(((NX - 1) * HALVES,)),
            dma(((NX - 1) * HALVES,)),
        ],
        compiler_params=pltpu.CompilerParams(
            collective_id=0, has_side_effects=True, vmem_limit_bytes=56 * 1024 * 1024
        ),
        name="layer",
    )(
        tokens,
        jnp.transpose(qkv_weight, (1, 0, 2)),
        out_weight.reshape(ny, NZ, slice_rows, model_width),
        prefix_state.reshape(nseq, slice_rows, hd),
    )


def solution(mesh):
    return jax.shard_map(
        on_device,
        mesh=mesh,
        in_specs=(
            P(("dp", "seq", "head"), None),
            P(None, None, "head"),
            P("head", None),
            P(("dp", "head"), None, None),
        ),
        out_specs=P(("dp", "seq", "head"), None),
        check_vma=False,
    )
```

```python
import functools

import jax
import jax.numpy as jnp
from jax import lax
from jax.experimental import pallas as pl
from jax.experimental.pallas import tpu as pltpu
from jax.sharding import PartitionSpec as P

MESH = pl.DeviceIdType.MESH
F32 = jnp.float32
BF16 = jnp.bfloat16

NZ = 8
NX = 4
PIECES = 4
HALVES = 2


class Ring:
    def __init__(self, block, me, n, sgn, device, send, recv, pieces=1):
        self.block, self.me, self.n, self.sgn = block, me, n, sgn
        self.device, self.send, self.recv = device, send, recv
        self.pieces = pieces
        self.far = n // 2
        self.near = n - 1 - self.far

    def at(self, steps):
        return lax.rem(self.me + self.sgn * steps + 2 * self.n, self.n)

    def hops(self, way):
        return self.far if way > 0 else self.near

    def sem(self, way, hop, piece):
        base = 0 if way > 0 else self.far
        return (base + hop) * self.pieces + piece

    def copy(self, way, hop, piece, src, dst):
        number = self.sem(way, hop, piece)
        return pltpu.make_async_remote_copy(
            src_ref=src,
            dst_ref=dst,
            send_sem=self.send.at[number],
            recv_sem=self.recv.at[number],
            device_id=self.device(self.at(way)),
            device_id_type=MESH,
        )

    def start(self, way, hop, piece=0, src=None):
        if hop < self.hops(way):
            here = self.block(-way * hop, self.at(-way * hop), piece)
            self.copy(way, hop, piece, here if src is None else src, self.landing(way, hop, piece)).start()

    def landing(self, way, hop, piece):
        return self.block(-way * (hop + 1), self.at(-way * hop), piece)

    def arrived(self, way, hop, piece=0):
        if hop < self.hops(way):
            here = self.block(-way * (hop + 1), self.at(-way * (hop + 1)), piece)
            self.copy(way, hop, piece, here, here).wait_recv()

    def pass_on(self, way, hop, piece=0):
        self.arrived(way, hop, piece)
        self.start(way, hop + 1, piece)

    def finish(self):
        for way in (1, -1):
            for hop in range(self.hops(way)):
                for piece in range(self.pieces):
                    here = self.block(-way * hop, self.at(-way * hop), piece)
                    self.copy(way, hop, piece, here, here).wait_send()


def kernel(
    ny,
    tok_hbm,
    wq_hbm,
    wo_hbm,
    prefix_hbm,
    out_ref,
    tok,
    wq,
    wo,
    qkv,
    st,
    off,
    mixed,
    nbuf,
    nrec,
    acc,
    sbuf,
    rbuf,
    pbuf,
    cbuf,
    prefix,
    lsem,
    tsend,
    trecv,
    xsend,
    xrecv,
    r1send,
    r1recv,
    r2send,
    r2recv,
    bsend,
    brecv,
    ssend,
    srecv,
    csend,
    crecv,
    nsend,
    nrecv,
):
    nseq = ny * NZ
    rows = tok.shape[1]
    heads = st.shape[1]
    hd = st.shape[2]
    width = wo.shape[-1]
    me = lax.axis_index("seq")
    mx = lax.axis_index("head")
    mc = lax.axis_index("dp")
    my = me // NZ
    mz = lax.rem(me, NZ)
    sgn = 1 - 2 * mc

    barrier = pltpu.get_barrier_semaphore()
    for step in range(1, NX):
        pl.semaphore_signal(
            barrier, inc=1, device_id={"head": lax.rem(mx + step, NX)}, device_id_type=MESH
        )
    pl.semaphore_signal(barrier, inc=1, device_id={"dp": 1 - mc}, device_id_type=MESH)

    for step in (1, NZ - 1):
        pl.semaphore_signal(
            barrier, inc=1, device_id={"seq": my * NZ + lax.rem(mz + step, NZ)}, device_id_type=MESH
        )
    for step in (1, ny - 1):
        pl.semaphore_signal(
            barrier, inc=1, device_id={"seq": lax.rem(my + step, ny) * NZ + mz}, device_id_type=MESH
        )
    loads = [pltpu.make_async_copy(tok_hbm, tok.at[0], lsem.at[0])]
    for part in range(3):
        loads.append(pltpu.make_async_copy(wq_hbm.at[part], wq.at[part], lsem.at[1 + part]))
    for band in range(4):
        loads.append(
            pltpu.make_async_copy(
                wo_hbm.at[:, :, :, pl.ds(band * width, width)], wo.at[band, 0], lsem.at[4 + band]
            )
        )
    loads.append(pltpu.make_async_copy(prefix_hbm.at[me], prefix, lsem.at[8]))
    for load in loads:
        load.start()

    pl.semaphore_wait(barrier, NX - 1 + 1 + 4)

    def slice_copy(side, step):
        band = mc * 2 + side
        number = side * (NX - 1) + step - 1
        return pltpu.make_async_remote_copy(
            src_ref=wo_hbm.at[my, mz, :, pl.ds(pl.multiple_of(band * width, width), width)],
            dst_ref=wo.at[band, NX - step, my, mz],
            send_sem=xsend.at[number],
            recv_sem=xrecv.at[number],
            device_id={"head": lax.rem(mx + step, NX)},
            device_id_type=MESH,
        )

    for side in range(2):
        for step in range(1, NX):
            slice_copy(side, step).start()

    prow = rows // PIECES

    loads[0].wait()

    def tok_copy(way, hop, piece, slot, landing):
        number = ((0 if way > 0 else 1) + 2 * hop) * PIECES + piece
        lower = piece * prow
        return pltpu.make_async_remote_copy(
            src_ref=tok.at[slot, pl.ds(lower, prow)],
            dst_ref=tok.at[landing, pl.ds(lower, prow)],
            send_sem=tsend.at[number],
            recv_sem=trecv.at[number],
            device_id={"head": lax.rem(mx + way + NX, NX)},
            device_id_type=MESH,
        )

    side_of = {1: NX - 1, -1: 1}
    middle = PIECES // 2
    passed = {1: range(middle), -1: range(middle, PIECES)}

    def tok_start(way, hop, piece):
        if hop == 0:
            tok_copy(way, 0, piece, 0, side_of[way]).start()
        else:
            tok_copy(way, 1, piece, side_of[way], 2).start()

    def tok_arrived(way, hop, piece):
        here = side_of[way] if hop == 0 else 2
        tok_copy(way, hop, piece, here, here).wait_recv()

    for step in range(PIECES):
        tok_start(1, 0, step)
        tok_start(-1, 0, (step + middle) % PIECES)

    def along_y(index):
        return {"seq": index * NZ + mz}

    def along_z(index):
        return {"seq": my * NZ + index}

    first = [
        Ring(
            lambda relative, index, piece: wo.at[mc * 2, pl.ds(1, NX - 1), index, mz],
            my, ny, sgn, along_y, r1send.at[0], r1recv.at[0],
        ),
        Ring(
            lambda relative, index, piece: wo.at[mc * 2 + 1, pl.ds(1, NX - 1), my, index],
            mz, NZ, sgn, along_z, r1send.at[1], r1recv.at[1],
        ),
    ]
    second = [
        Ring(
            lambda relative, index, piece: wo.at[mc * 2, pl.ds(1, NX - 1), :, index],
            mz, NZ, sgn, along_z, r2send.at[0], r2recv.at[0],
        ),
        Ring(
            lambda relative, index, piece: wo.at[mc * 2 + 1, pl.ds(1, NX - 1), index],
            my, ny, sgn, along_y, r2send.at[1], r2recv.at[1],
        ),
    ]

    def hop(ring, number):
        for way in (1, -1):
            ring.pass_on(way, number)

    def begin(ring):
        for way in (1, -1):
            ring.start(way, 0)

    def group_of(slot):
        return lax.rem(mx + slot, NX)

    def project(slot, first_part=0, parts=3, lower=0, count=rows):
        group = group_of(slot)
        pair = wq.shape[2] // 2

        def body(step, carry):
            part = step // 2
            side = lax.rem(step, 2)
            result = jnp.dot(
                tok[slot, pl.ds(lower, count)],
                wq[part, :, pl.ds(pl.multiple_of(side * pair, pair), pair)],
                preferred_element_type=F32,
            ).astype(BF16)
            for half in range(2):
                qkv[part * heads + side * 2 + half, group, pl.ds(lower, count)] = result[
                    :, half * hd : (half + 1) * hd
                ]
            return carry

        lax.fori_loop(2 * first_part, 2 * (first_part + parts), body, 0)

    def state(slot):
        group = group_of(slot)
        for head in range(heads):
            st[group, head] = lax.dot_general(
                qkv[heads + head, group],
                qkv[2 * heads + head, group],
                (((0,), (0,)), ((), ())),
                preferred_element_type=F32,
            )

    def slices_in(side):
        for step in range(1, NX):
            band = mc * 2 + side
            number = side * (NX - 1) + step - 1
            here = wo.at[band, NX - step, my, mz]
            pltpu.make_async_remote_copy(
                src_ref=here, dst_ref=here, send_sem=xsend.at[number], recv_sem=xrecv.at[number],
                device_id={"head": lax.rem(mx + step, NX)}, device_id_type=MESH,
            ).wait_recv()
        begin(first[side])

    for side in range(2):
        slices_in(side)
    for load in loads[1:4]:
        load.wait()
    project(0)
    hop(first[0], 0)
    hop(first[1], 0)
    hop(first[0], 1)
    begin(second[0])
    hop(first[1], 1)
    hop(first[1], 2)
    state(0)
    hop(first[1], 3)
    begin(second[1])
    hop(second[0], 0)
    for step in range(middle):
        for way in (1, -1):
            piece = passed[way][step]
            tok_arrived(way, 0, piece)
            tok_start(way, 1, piece)
    for way in (1, -1):
        for piece in passed[-way]:
            tok_arrived(way, 0, piece)
        project(side_of[way])
        if way > 0:
            hop(second[0], 1)
            hop(second[1], 0)
        state(side_of[way])
    hop(second[0], 2)

    def sibling(side):
        band = wo.at[mc * 2 + side, pl.ds(1, NX - 1)]
        return pltpu.make_async_remote_copy(
            src_ref=band, dst_ref=band, send_sem=bsend.at[side], recv_sem=brecv.at[side],
            device_id={"dp": 1 - mc}, device_id_type=MESH,
        )

    for way in (1, -1):
        for piece in passed[way]:
            tok_arrived(way, 1, piece)
    project(2, 1, 2)
    state(2)

    per_head = nseq // heads
    for head in range(heads):
        total = st[0, head] + st[1, head] + st[2, head] + st[3, head]
        sbuf[head * per_head : (head + 1) * per_head] = total.astype(BF16).reshape(
            per_head, hd // per_head, hd
        )

    def out_copy(step):
        to = lax.rem(me + step, nseq)
        return pltpu.make_async_remote_copy(
            src_ref=sbuf.at[to], dst_ref=rbuf.at[me], send_sem=ssend.at[0],
            recv_sem=srecv.at[0], device_id={"seq": to}, device_id_type=MESH,
        )

    def back_copy(step):
        to = lax.rem(me + step, nseq)
        return pltpu.make_async_remote_copy(
            src_ref=pbuf.at[to], dst_ref=cbuf.at[me], send_sem=csend.at[0],
            recv_sem=crecv.at[0], device_id={"seq": to}, device_id_type=MESH,
        )

    def all_of(source, target, send, recv):
        others = pl.ds(0, nseq - 1)
        return pltpu.make_async_remote_copy(
            src_ref=source.at[others], dst_ref=target.at[others], send_sem=send.at[0],
            recv_sem=recv.at[0], device_id={"seq": lax.rem(me + 1, nseq)}, device_id_type=MESH,
        )

    scattered = all_of(sbuf, rbuf, ssend, srecv)
    returned = all_of(pbuf, cbuf, csend, crecv)

    def hops_to(step):
        around_z, around_y = step % NZ, step // NZ
        return min(around_z, NZ - around_z) + min(around_y, ny - around_y)

    def far_first(action):
        for step in sorted(range(1, nseq), key=hops_to, reverse=True):
            action(step)

    far_first(lambda step: out_copy(step).start())
    rbuf[me] = sbuf[me]
    project(2, 0, 1)

    for head in range(heads):
        running = st[0, head]
        off[1, head] = running.astype(BF16)
        for group in range(2, NX):
            running = running + st[group - 1, head]
            off[group, head] = running.astype(BF16)
        off[0, head] = jnp.zeros((hd, hd), BF16)

    def inner(group):
        causal = lax.broadcasted_iota(jnp.int32, (rows, rows), 0) >= lax.broadcasted_iota(
            jnp.int32, (rows, rows), 1
        )
        for head in range(heads):
            query = qkv[head, group]
            scores = lax.dot_general(
                query, qkv[heads + head, group], (((1,), (1,)), ((), ())),
                preferred_element_type=F32,
            )
            weights = jnp.where(causal, scores, 0.0).astype(BF16)
            mixed[group, head] = jnp.dot(
                weights, qkv[2 * heads + head, group], preferred_element_type=F32
            ) + jnp.dot(query, off[group, head], preferred_element_type=F32)

    def inner_body(group, carry):
        inner(group)
        return carry

    lax.fori_loop(0, 1, inner_body, 0)

    scattered.wait_recv()
    loads[8].wait()
    total = prefix[...]
    for block in range(nseq):
        pbuf[block] = total.astype(BF16)
        if block < nseq - 1:
            total = total + rbuf[block].astype(F32)
    far_first(lambda step: back_copy(step).start())
    cbuf[me] = pbuf[me]
    hop(second[0], 3)
    hop(second[1], 1)
    for side in range(2):
        sibling(side).start()

    lax.fori_loop(1, NX, inner_body, 0)
    returned.wait_recv()

    hrow = rows // HALVES

    def normed_copy(step, half):
        number = (step - 1) * HALVES + half
        return pltpu.make_async_remote_copy(
            src_ref=nbuf.at[step, pl.ds(half * hrow, hrow)],
            dst_ref=nrec.at[NX - step - 1, pl.ds(half * hrow, hrow)],
            send_sem=nsend.at[number],
            recv_sem=nrecv.at[number],
            device_id={"head": lax.rem(mx + step, NX)},
            device_id_type=MESH,
        )

    def normed_in(step, half):
        number = (NX - step - 1) * HALVES + half
        here = nrec.at[step - 1, pl.ds(half * hrow, hrow)]
        return pltpu.make_async_remote_copy(
            src_ref=here, dst_ref=here, send_sem=nsend.at[number], recv_sem=nrecv.at[number],
            device_id={"head": lax.rem(mx + step, NX)}, device_id_type=MESH,
        )

    def normalize(step, half):
        group = lax.rem(mx + step, NX)
        lower = half * hrow
        for head in range(heads):
            carried = cbuf[head * per_head : (head + 1) * per_head].reshape(hd, hd)
            value = mixed[group, head, pl.ds(lower, hrow)] + jnp.dot(
                qkv[head, group, pl.ds(lower, hrow)], carried, preferred_element_type=F32
            )
            factor = lax.rsqrt(jnp.mean(value * value, axis=-1, keepdims=True) + 1e-06)
            nbuf[step, pl.ds(lower, hrow), head * hd : (head + 1) * hd] = (value * factor).astype(BF16)

    for half in range(HALVES):
        for step in (2, 1, 3):
            normalize(step, half)
            normed_copy(step, half).start()
    for half in range(HALVES):
        normalize(0, half)

    for load in loads[4:8]:
        load.wait()

    def weight(band, relative):
        return wo[band, relative].reshape(nseq * 16, width)

    def own(band, carry):
        columns = pl.ds(pl.multiple_of(band * width, width), width)
        acc[:, columns] = tok[0, :, columns].astype(F32) + jnp.dot(
            nbuf[0], weight(band, 0), preferred_element_type=F32
        )
        return carry

    lax.fori_loop(0, 4, own, 0)
    for side in range(2):
        band = wo.at[(1 - mc) * 2 + side, pl.ds(1, NX - 1)]
        pltpu.make_async_remote_copy(
            src_ref=band, dst_ref=band, send_sem=bsend.at[side], recv_sem=brecv.at[side],
            device_id={"dp": 1 - mc}, device_id_type=MESH,
        ).wait_recv()

    for half in range(HALVES):
        lower = half * hrow
        for place, step in enumerate((2, 1, 3)):
            normed_in(step, half).wait_recv()

            def project_out(band, carry):
                columns = pl.ds(pl.multiple_of(band * width, width), width)
                value = acc[lower : lower + hrow, columns] + jnp.dot(
                    nrec[step - 1, lower : lower + hrow], weight(band, step), preferred_element_type=F32
                )
                if place < 2:
                    acc[lower : lower + hrow, columns] = value
                else:
                    out_ref[pl.ds(lower, hrow), columns] = value.astype(BF16)
                return carry

            lax.fori_loop(0, 4, project_out, 0)

    for side in range(2):
        for step in range(1, NX):
            slice_copy(side, step).wait_send()
        sibling(side).wait_send()
    for ring in first + second:
        ring.finish()
    for way in (1, -1):
        for piece in range(PIECES):
            tok_copy(way, 0, piece, 0, side_of[way]).wait_send()
        for piece in passed[way]:
            tok_copy(way, 1, piece, side_of[way], 2).wait_send()
    scattered.wait_send()
    returned.wait_send()
    for step in range(1, NX):
        for half in range(HALVES):
            normed_copy(step, half).wait_send()


def on_device(tokens, qkv_weight, out_weight, prefix_state):
    rows, model_width = tokens.shape
    heads, hd, _ = prefix_state.shape
    group_width = heads * hd
    nseq = lax.axis_size("seq")
    ny = nseq // NZ
    width = model_width // 4
    slice_rows = group_width // nseq
    dma = pltpu.SemaphoreType.DMA
    return pl.pallas_call(
        functools.partial(kernel, ny),
        out_shape=jax.ShapeDtypeStruct((rows, model_width), BF16),
        in_specs=[pl.BlockSpec(memory_space=pl.ANY)] * 4,
        out_specs=pl.BlockSpec(memory_space=pltpu.VMEM),
        scratch_shapes=[
            pltpu.VMEM((NX, rows, model_width), BF16),
            pltpu.VMEM((3, model_width, group_width), BF16),
            pltpu.VMEM((4, NX, ny, NZ, slice_rows, width), BF16),
            pltpu.VMEM((3 * heads, NX, rows, hd), BF16),
            pltpu.VMEM((NX, heads, hd, hd), F32),
            pltpu.VMEM((NX, heads, hd, hd), BF16),
            pltpu.VMEM((NX, heads, rows, hd), F32),
            pltpu.VMEM((NX, rows, group_width), BF16),
            pltpu.VMEM((NX - 1, rows, group_width), BF16),
            pltpu.VMEM((rows, model_width), F32),
            pltpu.VMEM((nseq, slice_rows, hd), BF16),
            pltpu.VMEM((nseq, slice_rows, hd), BF16),
            pltpu.VMEM((nseq, slice_rows, hd), BF16),
            pltpu.VMEM((nseq, slice_rows, hd), BF16),
            pltpu.VMEM((slice_rows, hd), F32),
            dma((9,)),
            dma((4 * PIECES,)),
            dma((4 * PIECES,)),
            dma((2 * (NX - 1),)),
            dma((2 * (NX - 1),)),
            dma((2, NZ)),
            dma((2, NZ)),
            dma((2, NZ)),
            dma((2, NZ)),
            dma((2,)),
            dma((2,)),
            dma((1,)),
            dma((1,)),
            dma((1,)),
            dma((1,)),
            dma(((NX - 1) * HALVES,)),
            dma(((NX - 1) * HALVES,)),
        ],
        compiler_params=pltpu.CompilerParams(
            collective_id=0, has_side_effects=True, vmem_limit_bytes=34 * 1024 * 1024
        ),
        name="layer",
    )(
        *(
            pltpu.with_memory_space_constraint(operand, pltpu.HBM)
            for operand in (
                tokens,
                jnp.transpose(qkv_weight, (1, 0, 2)),
                out_weight.reshape(ny, NZ, slice_rows, model_width),
                prefix_state.reshape(nseq, slice_rows, hd),
            )
        )
    )


def solution(mesh):
    return jax.shard_map(
        on_device,
        mesh=mesh,
        in_specs=(
            P(("dp", "seq", "head"), None),
            P(None, None, "head"),
            P("head", None),
            P(("dp", "head"), None, None),
        ),
        out_specs=P(("dp", "seq", "head"), None),
        check_vma=False,
    )
```

```python
import functools

import jax
import jax.numpy as jnp
from jax import lax
from jax.experimental import pallas as pl
from jax.experimental.pallas import tpu as pltpu
from jax.sharding import PartitionSpec as P

MESH = pl.DeviceIdType.MESH
F32 = jnp.float32
BF16 = jnp.bfloat16

NZ = 8
NX = 4
PIECES = 4
HALVES = 2


class Ring:
    def __init__(self, block, me, n, sgn, device, send, recv, pieces=1):
        self.block, self.me, self.n, self.sgn = block, me, n, sgn
        self.device, self.send, self.recv = device, send, recv
        self.pieces = pieces
        self.far = n // 2
        self.near = n - 1 - self.far

    def at(self, steps):
        return lax.rem(self.me + self.sgn * steps + 2 * self.n, self.n)

    def hops(self, way):
        return self.far if way > 0 else self.near

    def sem(self, way, hop, piece):
        base = 0 if way > 0 else self.far
        return (base + hop) * self.pieces + piece

    def copy(self, way, hop, piece, src, dst):
        number = self.sem(way, hop, piece)
        return pltpu.make_async_remote_copy(
            src_ref=src,
            dst_ref=dst,
            send_sem=self.send.at[number],
            recv_sem=self.recv.at[number],
            device_id=self.device(self.at(way)),
            device_id_type=MESH,
        )

    def start(self, way, hop, piece=0, src=None):
        if hop < self.hops(way):
            here = self.block(-way * hop, self.at(-way * hop), piece)
            self.copy(way, hop, piece, here if src is None else src, self.landing(way, hop, piece)).start()

    def landing(self, way, hop, piece):
        return self.block(-way * (hop + 1), self.at(-way * hop), piece)

    def arrived(self, way, hop, piece=0):
        if hop < self.hops(way):
            here = self.block(-way * (hop + 1), self.at(-way * (hop + 1)), piece)
            self.copy(way, hop, piece, here, here).wait_recv()

    def pass_on(self, way, hop, piece=0):
        self.arrived(way, hop, piece)
        self.start(way, hop + 1, piece)

    def finish(self):
        for way in (1, -1):
            for hop in range(self.hops(way)):
                for piece in range(self.pieces):
                    here = self.block(-way * hop, self.at(-way * hop), piece)
                    self.copy(way, hop, piece, here, here).wait_send()


def kernel(
    ny,
    tok_hbm,
    wq_hbm,
    wo_hbm,
    prefix_hbm,
    out_ref,
    tok,
    wq,
    wo,
    qkv,
    st,
    off,
    mixed,
    nbuf,
    nrec,
    acc,
    sbuf,
    rbuf,
    pbuf,
    cbuf,
    prefix,
    lsem,
    tsend,
    trecv,
    xsend,
    xrecv,
    r1send,
    r1recv,
    r2send,
    r2recv,
    bsend,
    brecv,
    ssend,
    srecv,
    csend,
    crecv,
    nsend,
    nrecv,
):
    nseq = ny * NZ
    rows = tok.shape[1]
    heads = st.shape[1]
    hd = st.shape[2]
    width = wo.shape[-1]
    me = lax.axis_index("seq")
    mx = lax.axis_index("head")
    mc = lax.axis_index("dp")
    my = me // NZ
    mz = lax.rem(me, NZ)
    sgn = 1 - 2 * mc

    barrier = pltpu.get_barrier_semaphore()
    for step in range(1, NX):
        pl.semaphore_signal(
            barrier, inc=1, device_id={"head": lax.rem(mx + step, NX)}, device_id_type=MESH
        )
    pl.semaphore_signal(barrier, inc=1, device_id={"dp": 1 - mc}, device_id_type=MESH)

    for step in (1, NZ - 1):
        pl.semaphore_signal(
            barrier, inc=1, device_id={"seq": my * NZ + lax.rem(mz + step, NZ)}, device_id_type=MESH
        )
    for step in (1, ny - 1):
        pl.semaphore_signal(
            barrier, inc=1, device_id={"seq": lax.rem(my + step, ny) * NZ + mz}, device_id_type=MESH
        )
    loads = [pltpu.make_async_copy(tok_hbm, tok.at[0], lsem.at[0])]
    for part in range(3):
        loads.append(pltpu.make_async_copy(wq_hbm.at[part], wq.at[part], lsem.at[1 + part]))
    for band in range(4):
        loads.append(
            pltpu.make_async_copy(
                wo_hbm.at[:, :, :, pl.ds(band * width, width)], wo.at[band, 0], lsem.at[4 + band]
            )
        )
    loads.append(pltpu.make_async_copy(prefix_hbm.at[me], prefix, lsem.at[8]))
    for load in loads:
        load.start()

    pl.semaphore_wait(barrier, NX - 1 + 1 + 4)

    def slice_copy(side, step):
        band = mc * 2 + side
        number = side * (NX - 1) + step - 1
        return pltpu.make_async_remote_copy(
            src_ref=wo_hbm.at[my, mz, :, pl.ds(pl.multiple_of(band * width, width), width)],
            dst_ref=wo.at[band, NX - step, my, mz],
            send_sem=xsend.at[number],
            recv_sem=xrecv.at[number],
            device_id={"head": lax.rem(mx + step, NX)},
            device_id_type=MESH,
        )

    for side in range(2):
        for step in range(1, NX):
            slice_copy(side, step).start()

    prow = rows // PIECES

    def tok_copy(way, hop, piece, slot, landing):
        number = ((0 if way > 0 else 1) + 2 * hop) * PIECES + piece
        lower = piece * prow
        return pltpu.make_async_remote_copy(
            src_ref=tok.at[slot, pl.ds(lower, prow)],
            dst_ref=tok.at[landing, pl.ds(lower, prow)],
            send_sem=tsend.at[number],
            recv_sem=trecv.at[number],
            device_id={"head": lax.rem(mx + way + NX, NX)},
            device_id_type=MESH,
        )

    side_of = {1: NX - 1, -1: 1}
    middle = PIECES // 2
    passed = {1: range(middle), -1: range(middle, PIECES)}

    def tok_start(way, hop, piece):
        if hop == 0:
            number = (0 if way > 0 else 1) * PIECES + piece
            pltpu.make_async_remote_copy(
                src_ref=tok_hbm.at[pl.ds(piece * prow, prow)],
                dst_ref=tok.at[side_of[way], pl.ds(piece * prow, prow)],
                send_sem=tsend.at[number],
                recv_sem=trecv.at[number],
                device_id={"head": lax.rem(mx + way + NX, NX)},
                device_id_type=MESH,
            ).start()
        else:
            tok_copy(way, 1, piece, side_of[way], 2).start()

    def tok_arrived(way, hop, piece):
        here = side_of[way] if hop == 0 else 2
        tok_copy(way, hop, piece, here, here).wait_recv()

    for step in range(PIECES):
        tok_start(1, 0, step)
        tok_start(-1, 0, (step + middle) % PIECES)

    def along_y(index):
        return {"seq": index * NZ + mz}

    def along_z(index):
        return {"seq": my * NZ + index}

    first = [
        Ring(
            lambda relative, index, piece: wo.at[mc * 2, pl.ds(1, NX - 1), index, mz],
            my, ny, sgn, along_y, r1send.at[0], r1recv.at[0],
        ),
        Ring(
            lambda relative, index, piece: wo.at[mc * 2 + 1, pl.ds(1, NX - 1), my, index],
            mz, NZ, sgn, along_z, r1send.at[1], r1recv.at[1],
        ),
    ]
    second = [
        Ring(
            lambda relative, index, piece: wo.at[mc * 2, pl.ds(1, NX - 1), :, index],
            mz, NZ, sgn, along_z, r2send.at[0], r2recv.at[0],
        ),
        Ring(
            lambda relative, index, piece: wo.at[mc * 2 + 1, pl.ds(1, NX - 1), index],
            my, ny, sgn, along_y, r2send.at[1], r2recv.at[1],
        ),
    ]

    def to_sibling(ring, relative):
        side = second.index(ring)
        block = ring.block(relative, ring.at(relative), 0)
        pltpu.make_async_remote_copy(
            src_ref=block, dst_ref=block, send_sem=bsend.at[side], recv_sem=brecv.at[side],
            device_id={"dp": 1 - mc}, device_id_type=MESH,
        ).start()

    def hop(ring, number):
        for way in (1, -1):
            ring.pass_on(way, number)
        for way in (1, -1):
            if ring in second and number < ring.hops(way):
                to_sibling(ring, -way * (number + 1))

    def begin(ring):
        for way in (1, -1):
            ring.start(way, 0)
        if ring in second:
            to_sibling(ring, 0)

    def group_of(slot):
        return lax.rem(mx + slot, NX)

    def project(slot, first_part=0, parts=3, lower=0, count=rows):
        group = group_of(slot)
        pair = wq.shape[2] // 2

        def body(step, carry):
            part = step // 2
            side = lax.rem(step, 2)
            result = jnp.dot(
                tok[slot, pl.ds(lower, count)],
                wq[part, :, pl.ds(pl.multiple_of(side * pair, pair), pair)],
                preferred_element_type=F32,
            ).astype(BF16)
            for half in range(2):
                qkv[part * heads + side * 2 + half, group, pl.ds(lower, count)] = result[
                    :, half * hd : (half + 1) * hd
                ]
            return carry

        lax.fori_loop(2 * first_part, 2 * (first_part + parts), body, 0, unroll=parts == 2)

    def state(slot):
        group = group_of(slot)
        for head in range(heads):
            st[group, head] = lax.dot_general(
                qkv[heads + head, group],
                qkv[2 * heads + head, group],
                (((0,), (0,)), ((), ())),
                preferred_element_type=F32,
            )

    def slices_in(side):
        for step in range(1, NX):
            band = mc * 2 + side
            number = side * (NX - 1) + step - 1
            here = wo.at[band, NX - step, my, mz]
            pltpu.make_async_remote_copy(
                src_ref=here, dst_ref=here, send_sem=xsend.at[number], recv_sem=xrecv.at[number],
                device_id={"head": lax.rem(mx + step, NX)}, device_id_type=MESH,
            ).wait_recv()
        begin(first[side])

    for side in range(2):
        slices_in(side)
    for load in loads[:4]:
        load.wait()
    project(0)
    hop(first[0], 0)
    hop(first[1], 0)
    hop(first[0], 1)
    begin(second[0])
    hop(first[1], 1)
    hop(first[1], 2)
    state(0)
    hop(first[1], 3)
    begin(second[1])
    hop(second[0], 0)
    for step in range(middle):
        for way in (1, -1):
            piece = passed[way][step]
            tok_arrived(way, 0, piece)
            tok_start(way, 1, piece)
    for way in (1, -1):
        for piece in passed[-way]:
            tok_arrived(way, 0, piece)
        project(side_of[way])
        if way > 0:
            hop(second[0], 1)
            hop(second[1], 0)
        state(side_of[way])
    hop(second[0], 2)

    def sibling(side):
        band = wo.at[mc * 2 + side, pl.ds(1, NX - 1)]
        return pltpu.make_async_remote_copy(
            src_ref=band, dst_ref=band, send_sem=bsend.at[side], recv_sem=brecv.at[side],
            device_id={"dp": 1 - mc}, device_id_type=MESH,
        )

    for way in (1, -1):
        for piece in passed[way]:
            tok_arrived(way, 1, piece)
    project(2, 1, 2)
    state(2)

    per_head = nseq // heads
    for head in range(heads):
        total = st[0, head] + st[1, head] + st[2, head] + st[3, head]
        sbuf[head * per_head : (head + 1) * per_head] = total.astype(BF16).reshape(
            per_head, hd // per_head, hd
        )

    def out_copy(step):
        to = lax.rem(me + step, nseq)
        return pltpu.make_async_remote_copy(
            src_ref=sbuf.at[to], dst_ref=rbuf.at[me], send_sem=ssend.at[0],
            recv_sem=srecv.at[0], device_id={"seq": to}, device_id_type=MESH,
        )

    def back_copy(step):
        to = lax.rem(me + step, nseq)
        return pltpu.make_async_remote_copy(
            src_ref=pbuf.at[to], dst_ref=cbuf.at[me], send_sem=csend.at[0],
            recv_sem=crecv.at[0], device_id={"seq": to}, device_id_type=MESH,
        )

    def all_of(source, target, send, recv):
        others = pl.ds(0, nseq - 1)
        return pltpu.make_async_remote_copy(
            src_ref=source.at[others], dst_ref=target.at[others], send_sem=send.at[0],
            recv_sem=recv.at[0], device_id={"seq": lax.rem(me + 1, nseq)}, device_id_type=MESH,
        )

    scattered = all_of(sbuf, rbuf, ssend, srecv)
    returned = all_of(pbuf, cbuf, csend, crecv)

    def hops_to(step):
        around_z, around_y = step % NZ, step // NZ
        return min(around_z, NZ - around_z) + min(around_y, ny - around_y)

    def far_first(action):
        for step in sorted(range(1, nseq), key=hops_to, reverse=True):
            action(step)

    far_first(lambda step: out_copy(step).start())
    rbuf[me] = sbuf[me]
    project(2, 0, 1)

    for head in range(heads):
        running = st[0, head]
        off[1, head] = running.astype(BF16)
        for group in range(2, NX):
            running = running + st[group - 1, head]
            off[group, head] = running.astype(BF16)
        off[0, head] = jnp.zeros((hd, hd), BF16)

    def inner(group):
        causal = lax.broadcasted_iota(jnp.int32, (rows, rows), 0) >= lax.broadcasted_iota(
            jnp.int32, (rows, rows), 1
        )
        for head in range(heads):
            query = qkv[head, group]
            scores = lax.dot_general(
                query, qkv[heads + head, group], (((1,), (1,)), ((), ())),
                preferred_element_type=F32,
            )
            weights = jnp.where(causal, scores, 0.0).astype(BF16)
            mixed[group, head] = jnp.dot(
                weights, qkv[2 * heads + head, group], preferred_element_type=F32
            ) + jnp.dot(query, off[group, head], preferred_element_type=F32)

    def inner_body(group, carry):
        inner(group)
        return carry

    lax.fori_loop(0, 1, inner_body, 0)

    scattered.wait_recv()
    loads[8].wait()
    total = prefix[...]
    for block in range(nseq):
        pbuf[block] = total.astype(BF16)
        if block < nseq - 1:
            total = total + rbuf[block].astype(F32)
    far_first(lambda step: back_copy(step).start())
    cbuf[me] = pbuf[me]
    hop(second[0], 3)
    hop(second[1], 1)

    lax.fori_loop(1, NX, inner_body, 0)
    returned.wait_recv()

    hrow = rows // HALVES

    def normed_copy(step, half):
        number = (step - 1) * HALVES + half
        return pltpu.make_async_remote_copy(
            src_ref=nbuf.at[step, pl.ds(half * hrow, hrow)],
            dst_ref=nrec.at[NX - step - 1, pl.ds(half * hrow, hrow)],
            send_sem=nsend.at[number],
            recv_sem=nrecv.at[number],
            device_id={"head": lax.rem(mx + step, NX)},
            device_id_type=MESH,
        )

    def normed_in(step, half):
        number = (NX - step - 1) * HALVES + half
        here = nrec.at[step - 1, pl.ds(half * hrow, hrow)]
        return pltpu.make_async_remote_copy(
            src_ref=here, dst_ref=here, send_sem=nsend.at[number], recv_sem=nrecv.at[number],
            device_id={"head": lax.rem(mx + step, NX)}, device_id_type=MESH,
        )

    def normalize(step, half):
        group = lax.rem(mx + step, NX)
        lower = half * hrow
        for head in range(heads):
            carried = cbuf[head * per_head : (head + 1) * per_head].reshape(hd, hd)
            value = mixed[group, head, pl.ds(lower, hrow)] + jnp.dot(
                qkv[head, group, pl.ds(lower, hrow)], carried, preferred_element_type=F32
            )
            factor = lax.rsqrt(jnp.mean(value * value, axis=-1, keepdims=True) + 1e-06)
            nbuf[step, pl.ds(lower, hrow), head * hd : (head + 1) * hd] = (value * factor).astype(BF16)

    for half in range(HALVES):
        for step in (2, 1, 3):
            normalize(step, half)
            normed_copy(step, half).start()
    for half in range(HALVES):
        normalize(0, half)

    for load in loads[4:8]:
        load.wait()

    def weight(band, relative):
        return wo[band, relative].reshape(nseq * 16, width)

    def own(band, carry):
        columns = pl.ds(pl.multiple_of(band * width, width), width)
        acc[:, columns] = tok[0, :, columns].astype(F32) + jnp.dot(
            nbuf[0], weight(band, 0), preferred_element_type=F32
        )
        return carry

    lax.fori_loop(0, 4, own, 0, unroll=True)
    for side in range(2):
        band = wo.at[(1 - mc) * 2 + side, pl.ds(1, NX - 1)]
        pltpu.make_async_remote_copy(
            src_ref=band, dst_ref=band, send_sem=bsend.at[side], recv_sem=brecv.at[side],
            device_id={"dp": 1 - mc}, device_id_type=MESH,
        ).wait_recv()

    for half in range(HALVES):
        lower = half * hrow
        for place, step in enumerate((2, 1, 3)):
            normed_in(step, half).wait_recv()

            def project_out(band, carry):
                columns = pl.ds(pl.multiple_of(band * width, width), width)
                value = acc[lower : lower + hrow, columns] + jnp.dot(
                    nrec[step - 1, lower : lower + hrow], weight(band, step), preferred_element_type=F32
                )
                if place < 2:
                    acc[lower : lower + hrow, columns] = value
                else:
                    out_ref[pl.ds(lower, hrow), columns] = value.astype(BF16)
                return carry

            lax.fori_loop(0, 4, project_out, 0, unroll=True)

    for side in range(2):
        for step in range(1, NX):
            slice_copy(side, step).wait_send()
        sibling(side).wait_send()
    for ring in first + second:
        ring.finish()
    for way in (1, -1):
        for piece in range(PIECES):
            tok_copy(way, 0, piece, 0, side_of[way]).wait_send()
        for piece in passed[way]:
            tok_copy(way, 1, piece, side_of[way], 2).wait_send()
    scattered.wait_send()
    returned.wait_send()
    for step in range(1, NX):
        for half in range(HALVES):
            normed_copy(step, half).wait_send()


def on_device(tokens, qkv_weight, out_weight, prefix_state):
    rows, model_width = tokens.shape
    heads, hd, _ = prefix_state.shape
    group_width = heads * hd
    nseq = lax.axis_size("seq")
    ny = nseq // NZ
    width = model_width // 4
    slice_rows = group_width // nseq
    dma = pltpu.SemaphoreType.DMA
    return pl.pallas_call(
        functools.partial(kernel, ny),
        out_shape=jax.ShapeDtypeStruct((rows, model_width), BF16),
        in_specs=[pl.BlockSpec(memory_space=pl.ANY)] * 4,
        out_specs=pl.BlockSpec(memory_space=pltpu.VMEM),
        scratch_shapes=[
            pltpu.VMEM((NX, rows, model_width), BF16),
            pltpu.VMEM((3, model_width, group_width), BF16),
            pltpu.VMEM((4, NX, ny, NZ, slice_rows, width), BF16),
            pltpu.VMEM((3 * heads, NX, rows, hd), BF16),
            pltpu.VMEM((NX, heads, hd, hd), F32),
            pltpu.VMEM((NX, heads, hd, hd), BF16),
            pltpu.VMEM((NX, heads, rows, hd), F32),
            pltpu.VMEM((NX, rows, group_width), BF16),
            pltpu.VMEM((NX - 1, rows, group_width), BF16),
            pltpu.VMEM((rows, model_width), F32),
            pltpu.VMEM((nseq, slice_rows, hd), BF16),
            pltpu.VMEM((nseq, slice_rows, hd), BF16),
            pltpu.VMEM((nseq, slice_rows, hd), BF16),
            pltpu.VMEM((nseq, slice_rows, hd), BF16),
            pltpu.VMEM((slice_rows, hd), F32),
            dma((9,)),
            dma((4 * PIECES,)),
            dma((4 * PIECES,)),
            dma((2 * (NX - 1),)),
            dma((2 * (NX - 1),)),
            dma((2, NZ)),
            dma((2, NZ)),
            dma((2, NZ)),
            dma((2, NZ)),
            dma((2,)),
            dma((2,)),
            dma((1,)),
            dma((1,)),
            dma((1,)),
            dma((1,)),
            dma(((NX - 1) * HALVES,)),
            dma(((NX - 1) * HALVES,)),
        ],
        compiler_params=pltpu.CompilerParams(
            collective_id=0, has_side_effects=True, vmem_limit_bytes=34 * 1024 * 1024
        ),
        name="layer",
    )(
        *(
            pltpu.with_memory_space_constraint(operand, pltpu.HBM)
            for operand in (
                tokens,
                jnp.transpose(qkv_weight, (1, 0, 2)),
                out_weight.reshape(ny, NZ, slice_rows, model_width),
                prefix_state.reshape(nseq, slice_rows, hd),
            )
        )
    )


def solution(mesh):
    return jax.shard_map(
        on_device,
        mesh=mesh,
        in_specs=(
            P(("dp", "seq", "head"), None),
            P(None, None, "head"),
            P("head", None),
            P(("dp", "head"), None, None),
        ),
        out_specs=P(("dp", "seq", "head"), None),
        check_vma=False,
    )
```

```python
import functools

import jax
import jax.numpy as jnp
from jax import lax
from jax.experimental import pallas as pl
from jax.experimental.pallas import tpu as pltpu
from jax.sharding import PartitionSpec as P

MESH = pl.DeviceIdType.MESH
F32 = jnp.float32
BF16 = jnp.bfloat16

NZ = 8
NX = 4
PIECES = 4
HALVES = 2


class Ring:
    def __init__(self, block, me, n, sgn, device, send, recv, pieces=1):
        self.block, self.me, self.n, self.sgn = block, me, n, sgn
        self.device, self.send, self.recv = device, send, recv
        self.pieces = pieces
        self.far = n // 2
        self.near = n - 1 - self.far

    def at(self, steps):
        return lax.rem(self.me + self.sgn * steps + 2 * self.n, self.n)

    def hops(self, way):
        return self.far if way > 0 else self.near

    def sem(self, way, hop, piece):
        base = 0 if way > 0 else self.far
        return (base + hop) * self.pieces + piece

    def copy(self, way, hop, piece, src, dst):
        number = self.sem(way, hop, piece)
        return pltpu.make_async_remote_copy(
            src_ref=src,
            dst_ref=dst,
            send_sem=self.send.at[number],
            recv_sem=self.recv.at[number],
            device_id=self.device(self.at(way)),
            device_id_type=MESH,
        )

    def start(self, way, hop, piece=0, src=None):
        if hop < self.hops(way):
            here = self.block(-way * hop, self.at(-way * hop), piece)
            self.copy(way, hop, piece, here if src is None else src, self.landing(way, hop, piece)).start()

    def landing(self, way, hop, piece):
        return self.block(-way * (hop + 1), self.at(-way * hop), piece)

    def arrived(self, way, hop, piece=0):
        if hop < self.hops(way):
            here = self.block(-way * (hop + 1), self.at(-way * (hop + 1)), piece)
            self.copy(way, hop, piece, here, here).wait_recv()

    def pass_on(self, way, hop, piece=0):
        self.arrived(way, hop, piece)
        self.start(way, hop + 1, piece)

    def finish(self):
        for way in (1, -1):
            for hop in range(self.hops(way)):
                for piece in range(self.pieces):
                    here = self.block(-way * hop, self.at(-way * hop), piece)
                    self.copy(way, hop, piece, here, here).wait_send()


def kernel(
    ny,
    tok_hbm,
    wq_hbm,
    wo_hbm,
    prefix_hbm,
    out_ref,
    tok,
    wq,
    wo,
    qkv,
    st,
    off,
    mixed,
    nbuf,
    nrec,
    acc,
    sbuf,
    rbuf,
    pbuf,
    cbuf,
    prefix,
    lsem,
    tsend,
    trecv,
    xsend,
    xrecv,
    r1send,
    r1recv,
    r2send,
    r2recv,
    bsend,
    brecv,
    ssend,
    srecv,
    csend,
    crecv,
    nsend,
    nrecv,
):
    nseq = ny * NZ
    rows = tok.shape[1]
    heads = st.shape[1]
    hd = st.shape[2]
    width = wo.shape[-1]
    me = lax.axis_index("seq")
    mx = lax.axis_index("head")
    mc = lax.axis_index("dp")
    my = me // NZ
    mz = lax.rem(me, NZ)
    sgn = 1 - 2 * mc

    barrier = pltpu.get_barrier_semaphore()
    for step in range(1, NX):
        pl.semaphore_signal(
            barrier, inc=1, device_id={"head": lax.rem(mx + step, NX)}, device_id_type=MESH
        )
    pl.semaphore_signal(barrier, inc=1, device_id={"dp": 1 - mc}, device_id_type=MESH)

    for step in (1, NZ - 1):
        pl.semaphore_signal(
            barrier, inc=1, device_id={"seq": my * NZ + lax.rem(mz + step, NZ)}, device_id_type=MESH
        )
    for step in (1, ny - 1):
        pl.semaphore_signal(
            barrier, inc=1, device_id={"seq": lax.rem(my + step, ny) * NZ + mz}, device_id_type=MESH
        )
    loads = [pltpu.make_async_copy(tok_hbm, tok.at[0], lsem.at[0])]
    for part in range(3):
        loads.append(pltpu.make_async_copy(wq_hbm.at[part], wq.at[part], lsem.at[1 + part]))
    for band in range(4):
        loads.append(
            pltpu.make_async_copy(
                wo_hbm.at[:, :, :, pl.ds(band * width, width)], wo.at[band, 0], lsem.at[4 + band]
            )
        )
    loads.append(pltpu.make_async_copy(prefix_hbm.at[me], prefix, lsem.at[8]))
    for load in loads:
        load.start()

    pl.semaphore_wait(barrier, NX - 1 + 1 + 4)

    def slice_copy(side, step):
        band = mc * 2 + side
        number = side * (NX - 1) + step - 1
        return pltpu.make_async_remote_copy(
            src_ref=wo_hbm.at[my, mz, :, pl.ds(pl.multiple_of(band * width, width), width)],
            dst_ref=wo.at[band, NX - step, my, mz],
            send_sem=xsend.at[number],
            recv_sem=xrecv.at[number],
            device_id={"head": lax.rem(mx + step, NX)},
            device_id_type=MESH,
        )

    for side in range(2):
        for step in range(1, NX):
            slice_copy(side, step).start()

    prow = rows // PIECES

    def tok_copy(way, hop, piece, slot, landing):
        number = ((0 if way > 0 else 1) + 2 * hop) * PIECES + piece
        lower = piece * prow
        return pltpu.make_async_remote_copy(
            src_ref=tok.at[slot, pl.ds(lower, prow)],
            dst_ref=tok.at[landing, pl.ds(lower, prow)],
            send_sem=tsend.at[number],
            recv_sem=trecv.at[number],
            device_id={"head": lax.rem(mx + way + NX, NX)},
            device_id_type=MESH,
        )

    side_of = {1: NX - 1, -1: 1}
    middle = PIECES // 2
    passed = {1: range(0, PIECES, 2), -1: range(1, PIECES, 2)}

    def tok_start(way, hop, piece):
        if hop == 0:
            number = (0 if way > 0 else 1) * PIECES + piece
            pltpu.make_async_remote_copy(
                src_ref=tok_hbm.at[pl.ds(piece * prow, prow)],
                dst_ref=tok.at[side_of[way], pl.ds(piece * prow, prow)],
                send_sem=tsend.at[number],
                recv_sem=trecv.at[number],
                device_id={"head": lax.rem(mx + way + NX, NX)},
                device_id_type=MESH,
            ).start()
        else:
            tok_copy(way, 1, piece, side_of[way], 2).start()

    def tok_arrived(way, hop, piece):
        here = side_of[way] if hop == 0 else 2
        tok_copy(way, hop, piece, here, here).wait_recv()

    for step in range(PIECES):
        for way in (1, -1):
            tok_start(way, 0, (*passed[way], *passed[-way])[step])

    def along_y(index):
        return {"seq": index * NZ + mz}

    def along_z(index):
        return {"seq": my * NZ + index}

    first = [
        Ring(
            lambda relative, index, piece: wo.at[mc * 2, pl.ds(1, NX - 1), index, mz],
            my, ny, sgn, along_y, r1send.at[0], r1recv.at[0],
        ),
        Ring(
            lambda relative, index, piece: wo.at[mc * 2 + 1, pl.ds(1, NX - 1), my, index],
            mz, NZ, sgn, along_z, r1send.at[1], r1recv.at[1],
        ),
    ]
    second = [
        Ring(
            lambda relative, index, piece: wo.at[mc * 2, pl.ds(1, NX - 1), :, index],
            mz, NZ, sgn, along_z, r2send.at[0], r2recv.at[0],
        ),
        Ring(
            lambda relative, index, piece: wo.at[mc * 2 + 1, pl.ds(1, NX - 1), index],
            my, ny, sgn, along_y, r2send.at[1], r2recv.at[1],
        ),
    ]

    def to_sibling(ring, relative):
        side = second.index(ring)
        block = ring.block(relative, ring.at(relative), 0)
        pltpu.make_async_remote_copy(
            src_ref=block, dst_ref=block, send_sem=bsend.at[side], recv_sem=brecv.at[side],
            device_id={"dp": 1 - mc}, device_id_type=MESH,
        ).start()

    def hop(ring, number):
        for way in (1, -1):
            ring.pass_on(way, number)
        for way in (1, -1):
            if ring in second and number < ring.hops(way):
                to_sibling(ring, -way * (number + 1))

    def begin(ring):
        for way in (1, -1):
            ring.start(way, 0)
        if ring in second:
            to_sibling(ring, 0)

    def group_of(slot):
        return lax.rem(mx + slot, NX)

    def project(slot, first_part=0, parts=3, lower=0, count=rows):
        group = group_of(slot)
        pair = wq.shape[2] // 2

        def body(step, carry):
            part = step // 2
            side = lax.rem(step, 2)
            result = jnp.dot(
                tok[slot, pl.ds(lower, count)],
                wq[part, :, pl.ds(pl.multiple_of(side * pair, pair), pair)],
                preferred_element_type=F32,
            ).astype(BF16)
            for half in range(2):
                qkv[part * heads + side * 2 + half, group, pl.ds(lower, count)] = result[
                    :, half * hd : (half + 1) * hd
                ]
            return carry

        lax.fori_loop(2 * first_part, 2 * (first_part + parts), body, 0, unroll=parts == 2)

    def state(slot):
        group = group_of(slot)
        for head in range(heads):
            st[group, head] = lax.dot_general(
                qkv[heads + head, group],
                qkv[2 * heads + head, group],
                (((0,), (0,)), ((), ())),
                preferred_element_type=F32,
            )

    def slices_in(side):
        for step in range(1, NX):
            band = mc * 2 + side
            number = side * (NX - 1) + step - 1
            here = wo.at[band, NX - step, my, mz]
            pltpu.make_async_remote_copy(
                src_ref=here, dst_ref=here, send_sem=xsend.at[number], recv_sem=xrecv.at[number],
                device_id={"head": lax.rem(mx + step, NX)}, device_id_type=MESH,
            ).wait_recv()
        begin(first[side])

    for side in range(2):
        slices_in(side)
    for load in loads[:4]:
        load.wait()
    project(0)
    hop(first[0], 0)
    hop(first[1], 0)
    hop(first[0], 1)
    begin(second[0])
    hop(first[1], 1)
    hop(first[1], 2)
    state(0)
    hop(first[1], 3)
    begin(second[1])
    hop(second[0], 0)
    for step in range(middle):
        for way in (1, -1):
            piece = passed[way][step]
            tok_arrived(way, 0, piece)
            tok_start(way, 1, piece)
    for way in (1, -1):
        for piece in passed[-way]:
            tok_arrived(way, 0, piece)
        project(side_of[way])
        if way > 0:
            hop(second[0], 1)
            hop(second[1], 0)
        state(side_of[way])
    hop(second[0], 2)

    def sibling(side):
        band = wo.at[mc * 2 + side, pl.ds(1, NX - 1)]
        return pltpu.make_async_remote_copy(
            src_ref=band, dst_ref=band, send_sem=bsend.at[side], recv_sem=brecv.at[side],
            device_id={"dp": 1 - mc}, device_id_type=MESH,
        )

    for wave in range(middle):
        for way in (1, -1):
            tok_arrived(way, 1, passed[way][wave])
        project(2, 1, 2, wave * 2 * prow, 2 * prow)
    state(2)

    per_head = nseq // heads
    for head in range(heads):
        total = st[0, head] + st[1, head] + st[2, head] + st[3, head]
        sbuf[head * per_head : (head + 1) * per_head] = total.astype(BF16).reshape(
            per_head, hd // per_head, hd
        )

    def out_copy(step):
        to = lax.rem(me + step, nseq)
        return pltpu.make_async_remote_copy(
            src_ref=sbuf.at[to], dst_ref=rbuf.at[me], send_sem=ssend.at[0],
            recv_sem=srecv.at[0], device_id={"seq": to}, device_id_type=MESH,
        )

    def back_copy(step):
        to = lax.rem(me + step, nseq)
        return pltpu.make_async_remote_copy(
            src_ref=pbuf.at[to], dst_ref=cbuf.at[me], send_sem=csend.at[0],
            recv_sem=crecv.at[0], device_id={"seq": to}, device_id_type=MESH,
        )

    def all_of(source, target, send, recv):
        others = pl.ds(0, nseq - 1)
        return pltpu.make_async_remote_copy(
            src_ref=source.at[others], dst_ref=target.at[others], send_sem=send.at[0],
            recv_sem=recv.at[0], device_id={"seq": lax.rem(me + 1, nseq)}, device_id_type=MESH,
        )

    scattered = all_of(sbuf, rbuf, ssend, srecv)
    returned = all_of(pbuf, cbuf, csend, crecv)

    def hops_to(step):
        around_z, around_y = step % NZ, step // NZ
        return min(around_z, NZ - around_z) + min(around_y, ny - around_y)

    def far_first(action):
        for step in sorted(range(1, nseq), key=hops_to, reverse=True):
            action(step)

    far_first(lambda step: out_copy(step).start())
    rbuf[me] = sbuf[me]
    project(2, 0, 1)

    for head in range(heads):
        running = st[0, head]
        off[1, head] = running.astype(BF16)
        for group in range(2, NX):
            running = running + st[group - 1, head]
            off[group, head] = running.astype(BF16)
        off[0, head] = jnp.zeros((hd, hd), BF16)

    def inner(group):
        causal = lax.broadcasted_iota(jnp.int32, (rows, rows), 0) >= lax.broadcasted_iota(
            jnp.int32, (rows, rows), 1
        )
        for head in range(heads):
            query = qkv[head, group]
            scores = lax.dot_general(
                query, qkv[heads + head, group], (((1,), (1,)), ((), ())),
                preferred_element_type=F32,
            )
            weights = jnp.where(causal, scores, 0.0).astype(BF16)
            mixed[group, head] = jnp.dot(
                weights, qkv[2 * heads + head, group], preferred_element_type=F32
            ) + jnp.dot(query, off[group, head], preferred_element_type=F32)

    def inner_body(group, carry):
        inner(group)
        return carry

    lax.fori_loop(0, 1, inner_body, 0)

    scattered.wait_recv()
    loads[8].wait()
    total = prefix[...]
    for block in range(nseq):
        pbuf[block] = total.astype(BF16)

        @pl.when(block != me)
        def _():
            pltpu.make_async_remote_copy(
                src_ref=pbuf.at[block], dst_ref=cbuf.at[me], send_sem=csend.at[0],
                recv_sem=crecv.at[0], device_id={"seq": block}, device_id_type=MESH,
            ).start()

        if block < nseq - 1:
            total = total + rbuf[block].astype(F32)
    cbuf[me] = pbuf[me]
    hop(second[0], 3)
    hop(second[1], 1)

    lax.fori_loop(1, NX, inner_body, 0)
    returned.wait_recv()

    hrow = rows // HALVES

    def normed_copy(step, half):
        number = (step - 1) * HALVES + half
        return pltpu.make_async_remote_copy(
            src_ref=nbuf.at[step, pl.ds(half * hrow, hrow)],
            dst_ref=nrec.at[NX - step - 1, pl.ds(half * hrow, hrow)],
            send_sem=nsend.at[number],
            recv_sem=nrecv.at[number],
            device_id={"head": lax.rem(mx + step, NX)},
            device_id_type=MESH,
        )

    def normed_in(step, half):
        number = (NX - step - 1) * HALVES + half
        here = nrec.at[step - 1, pl.ds(half * hrow, hrow)]
        return pltpu.make_async_remote_copy(
            src_ref=here, dst_ref=here, send_sem=nsend.at[number], recv_sem=nrecv.at[number],
            device_id={"head": lax.rem(mx + step, NX)}, device_id_type=MESH,
        )

    def normalize(step, half):
        group = lax.rem(mx + step, NX)
        lower = half * hrow
        for head in range(heads):
            carried = cbuf[head * per_head : (head + 1) * per_head].reshape(hd, hd)
            value = mixed[group, head, pl.ds(lower, hrow)] + jnp.dot(
                qkv[head, group, pl.ds(lower, hrow)], carried, preferred_element_type=F32
            )
            factor = lax.rsqrt(jnp.mean(value * value, axis=-1, keepdims=True) + 1e-06)
            nbuf[step, pl.ds(lower, hrow), head * hd : (head + 1) * hd] = (value * factor).astype(BF16)

    for half in range(HALVES):
        for step in (2, 1, 3):
            normalize(step, half)
            normed_copy(step, half).start()
    for half in range(HALVES):
        normalize(0, half)

    for load in loads[4:8]:
        load.wait()

    def weight(band, relative):
        return wo[band, relative].reshape(nseq * 16, width)

    def own(band, carry):
        columns = pl.ds(pl.multiple_of(band * width, width), width)
        acc[:, columns] = tok[0, :, columns].astype(F32) + jnp.dot(
            nbuf[0], weight(band, 0), preferred_element_type=F32
        )
        return carry

    lax.fori_loop(0, 4, own, 0, unroll=True)
    for side in range(2):
        band = wo.at[(1 - mc) * 2 + side, pl.ds(1, NX - 1)]
        pltpu.make_async_remote_copy(
            src_ref=band, dst_ref=band, send_sem=bsend.at[side], recv_sem=brecv.at[side],
            device_id={"dp": 1 - mc}, device_id_type=MESH,
        ).wait_recv()

    for half in range(HALVES):
        lower = half * hrow
        for place, step in enumerate((2, 1, 3)):
            normed_in(step, half).wait_recv()

            def project_out(band, carry):
                columns = pl.ds(pl.multiple_of(band * width, width), width)
                value = acc[lower : lower + hrow, columns] + jnp.dot(
                    nrec[step - 1, lower : lower + hrow], weight(band, step), preferred_element_type=F32
                )
                if place < 2:
                    acc[lower : lower + hrow, columns] = value
                else:
                    out_ref[pl.ds(lower, hrow), columns] = value.astype(BF16)
                return carry

            lax.fori_loop(0, 4, project_out, 0, unroll=True)

    for side in range(2):
        for step in range(1, NX):
            slice_copy(side, step).wait_send()
        sibling(side).wait_send()
    for ring in first + second:
        ring.finish()
    for way in (1, -1):
        for piece in range(PIECES):
            tok_copy(way, 0, piece, 0, side_of[way]).wait_send()
        for piece in passed[way]:
            tok_copy(way, 1, piece, side_of[way], 2).wait_send()
    scattered.wait_send()
    returned.wait_send()
    for step in range(1, NX):
        for half in range(HALVES):
            normed_copy(step, half).wait_send()


def on_device(tokens, qkv_weight, out_weight, prefix_state):
    rows, model_width = tokens.shape
    heads, hd, _ = prefix_state.shape
    group_width = heads * hd
    nseq = lax.axis_size("seq")
    ny = nseq // NZ
    width = model_width // 4
    slice_rows = group_width // nseq
    dma = pltpu.SemaphoreType.DMA
    return pl.pallas_call(
        functools.partial(kernel, ny),
        out_shape=jax.ShapeDtypeStruct((rows, model_width), BF16),
        in_specs=[pl.BlockSpec(memory_space=pl.ANY)] * 4,
        out_specs=pl.BlockSpec(memory_space=pltpu.VMEM),
        scratch_shapes=[
            pltpu.VMEM((NX, rows, model_width), BF16),
            pltpu.VMEM((3, model_width, group_width), BF16),
            pltpu.VMEM((4, NX, ny, NZ, slice_rows, width), BF16),
            pltpu.VMEM((3 * heads, NX, rows, hd), BF16),
            pltpu.VMEM((NX, heads, hd, hd), F32),
            pltpu.VMEM((NX, heads, hd, hd), BF16),
            pltpu.VMEM((NX, heads, rows, hd), F32),
            pltpu.VMEM((NX, rows, group_width), BF16),
            pltpu.VMEM((NX - 1, rows, group_width), BF16),
            pltpu.VMEM((rows, model_width), F32),
            pltpu.VMEM((nseq, slice_rows, hd), BF16),
            pltpu.VMEM((nseq, slice_rows, hd), BF16),
            pltpu.VMEM((nseq, slice_rows, hd), BF16),
            pltpu.VMEM((nseq, slice_rows, hd), BF16),
            pltpu.VMEM((slice_rows, hd), F32),
            dma((9,)),
            dma((4 * PIECES,)),
            dma((4 * PIECES,)),
            dma((2 * (NX - 1),)),
            dma((2 * (NX - 1),)),
            dma((2, NZ)),
            dma((2, NZ)),
            dma((2, NZ)),
            dma((2, NZ)),
            dma((2,)),
            dma((2,)),
            dma((1,)),
            dma((1,)),
            dma((1,)),
            dma((1,)),
            dma(((NX - 1) * HALVES,)),
            dma(((NX - 1) * HALVES,)),
        ],
        compiler_params=pltpu.CompilerParams(
            collective_id=0, has_side_effects=True, vmem_limit_bytes=34 * 1024 * 1024
        ),
        name="layer",
    )(
        *(
            pltpu.with_memory_space_constraint(operand, pltpu.HBM)
            for operand in (
                tokens,
                jnp.transpose(qkv_weight, (1, 0, 2)),
                out_weight.reshape(ny, NZ, slice_rows, model_width),
                prefix_state.reshape(nseq, slice_rows, hd),
            )
        )
    )


def solution(mesh):
    return jax.shard_map(
        on_device,
        mesh=mesh,
        in_specs=(
            P(("dp", "seq", "head"), None),
            P(None, None, "head"),
            P("head", None),
            P(("dp", "head"), None, None),
        ),
        out_specs=P(("dp", "seq", "head"), None),
        check_vma=False,
    )
```
